32 devices in a mesh: grp: 2 (over y), elem: 4 (over z), src: 2 (over x), sub: 2 (over core).
Axes of the slice: x: 2, y: 2, z: 4, core: 2. Of those that a mesh axis runs over, the one named last changes fastest.
Arguments:
- trace_rhs: bfloat16 [6144, 2048], P(('grp', 'elem', 'sub'), 'src'), parts along dimension 0, may hold values from -6 to 6
- face_scale: float32 [6144], P(('grp', 'elem', 'sub')), parts along dimension 0, may hold values from 0.5 to 2
- stiff_scale: float32 [2048], P(('grp', 'elem', 'sub')), parts along dimension 0, may hold values from 0.25 to 1
- mass_scale: float32 [2048], P(('grp', 'elem', 'sub')), parts along dimension 0, may hold values from 0.1 to 0.5
- elem_faces: int32 [2048, 6], P(('grp', 'elem', 'sub')), parts along dimension 0, may hold values from 0 to 479, as said below
- halo_faces: int32 [16, 3, 32], P(('grp', 'elem', 'sub')), parts along dimension 0, may hold values from 0 to 383
- elem_count: int32 [16], P(('grp', 'elem', 'sub')), parts along dimension 0, may hold values from 16 to 128, as said below
- jacobi_block: bfloat16 [64, 64], replicated, may hold values from -0.75 to 0.75
- stiffness: bfloat16 [384, 384], replicated, may hold values from -0.3125 to 0.3125
- mass: bfloat16 [384, 384], replicated, may hold values from -0.3125 to 0.3125
- lifting: bfloat16 [384, 512], replicated, may hold values from -0.3125 to 0.3125
Outputs:
- applied: bfloat16 [6144, 2048], P(('grp', 'elem', 'sub'), 'src'), parts along dimension 0
- interior: bfloat16 [2048, 16384], P(('grp', 'elem', 'sub'), 'src'), parts along dimension 0
The draws below stay inside these ranges and needn't reach their ends.
There are 2 independent parts, one for each index of `grp`. The reference program is written for one: setup_inputs(seed, part) draws one part's arguments, and reference() takes and returns one part's arrays. A program takes and returns all parts, laid end to end along the dimension named above; an argument that names none is the same for every part. Nothing has to cross between parts.
Inputs may be any that keep to these rules, and one draw needn't show every extreme that they name: `elem_faces`: each element's six entries index owned faces of its own partition or halo slots toward neighbours that exist (partitions 0 to 7). `elem_count`: A multiple of 16; some partition is full in every draw.
All inputs are finite; a program needn't handle non-finite values.
Results may differ from the reference program's by a relative error of at most 0.0065.
Values may be sent and summed in bfloat16 or wider, within the bound.
No kernel may reach another device: no remote copies, remote signals or barrier semaphores. Data moves between devices by JAX's collectives and lax.ppermute only.
A program may use at most 64 MiB of HBM per device.

```python
import math
import jax
import jax.numpy as jnp
from jax import lax

FD = 64
ELD = 384
NI = 512
EBLK = 16
E_DEV = 128
H = 32
F_DEV = 384
PARTITIONS = 8
ELEMENTS = 1024
FACES = 3072
NSRC = 32
N_ELEM = 4
N_SUB = 2


def draw_elem_faces(key, part):
    key_local, key_dir, key_slot, key_pick = jax.random.split(key, 4)
    owned = jax.random.randint(key_local, (ELEMENTS, 6), 0, F_DEV)
    direction = jax.random.randint(key_dir, (ELEMENTS, 6), 0, 3)
    part_ids = (jnp.arange(ELEMENTS) // E_DEV)[:, None]
    elem_pos = part_ids // N_SUB
    missing = (direction == 0) & (elem_pos == 0) | (direction == 1) & (elem_pos == N_ELEM - 1)
    direction = jnp.where(missing, 2, direction)
    slot = jax.random.randint(key_slot, (ELEMENTS, 6), 0, H)
    remote = F_DEV + direction * H + slot
    picker = jax.random.randint(key_pick, (ELEMENTS, 6), 0, 3)
    chosen = jnp.where(picker == 0, remote, owned)
    chosen = chosen.at[0, 0].set(F_DEV + 3 * H - 1)
    chosen = chosen.at[0, 1].set(0)
    return chosen.astype(jnp.int32)


def draw_elem_count(key, part):
    key_count, key_full = jax.random.split(key, 2)
    blocks = jax.random.randint(key_count, (PARTITIONS,), 1, E_DEV // EBLK + 1)
    fullest = jax.random.randint(key_full, (), 0, PARTITIONS)
    blocks = jnp.where(jnp.arange(PARTITIONS) == fullest, E_DEV // EBLK, blocks)
    return (blocks * EBLK).astype(jnp.int32)


def plant(array, own_key, low, largest):
    longest = array.shape.index(max(array.shape))
    spots = []
    for shift in (0, 1):
        where = [jax.random.randint(jax.random.fold_in(own_key, axis), (), 0, length) for axis, length in enumerate(array.shape)]
        where[longest] = (where[longest] + shift) % array.shape[longest]
        spots.append(tuple(where))
    return array.at[spots[0]].set(low).at[spots[1]].set(largest)


def block_scale(own_key, shape, cuts, smallest, high):
    def one(axis_at, blocks):
        steps = jax.random.uniform(jax.random.fold_in(jax.random.fold_in(own_key, 6), axis_at), (blocks,), jnp.float32, smallest / len(cuts), high / len(cuts))
        return jnp.repeat(jnp.exp(steps), shape[axis_at] // blocks).reshape((-1,) + (1,) * (len(shape) - axis_at - 1))

    loudness = one(*cuts[0])
    for cut in cuts[1:]:
        loudness = loudness * one(*cut)
    return loudness


def centred(own_key, extent, deviation, bound, cuts=(), kind=jnp.bfloat16):
    values = jax.random.normal(own_key, extent, jnp.float32) * deviation
    if len(cuts) > 0:
        values = block_scale(own_key, extent, cuts, -0.22, 0.18) * values
    return jnp.clip(values, min=-bound, max=bound).astype(kind)


def setup_inputs(seed: int = 0, part: int = 0) -> dict:
    keys = jax.random.split(jax.random.key(seed), 12)
    part_keys = jax.random.split(jax.random.fold_in(keys[11], part), 12)
    trace_rhs = centred(part_keys[0], (FACES, NSRC * FD), 1.0, 6.0, ((0, 8), (1, 2)))
    face_scale = jnp.clip(jnp.exp(math.log(2.0) - 1.3862944 * jax.random.uniform(part_keys[1], (FACES,), jnp.float32) ** block_scale(part_keys[1], (FACES,), ((0, 8),), -0.2, 0.2)), 0.5, 2.0)
    stiff_scale = jnp.clip(jnp.exp(math.log(1.0) - 1.3862944 * jax.random.uniform(part_keys[2], (ELEMENTS,), jnp.float32) ** block_scale(part_keys[2], (ELEMENTS,), ((0, 8),), -0.2, 0.2)), 0.25, 1.0)
    mass_scale = jnp.clip(jnp.exp(math.log(0.5) - 1.609438 * jax.random.uniform(part_keys[3], (ELEMENTS,), jnp.float32) ** block_scale(part_keys[3], (ELEMENTS,), ((0, 8),), -0.2, 0.2)), 0.1, 0.5)
    elem_faces = draw_elem_faces(jax.random.fold_in(jax.random.fold_in(keys[11], part), 71), part)
    halo_faces = plant(jax.random.randint(part_keys[5], (PARTITIONS, 3, H), 0, F_DEV), jax.random.fold_in(part_keys[5], 1), 0, F_DEV - 1).astype(jnp.int32)
    elem_count = draw_elem_count(jax.random.fold_in(jax.random.fold_in(keys[11], part), 71), part)
    jacobi_block = centred(keys[7], (FD, FD), FD ** -0.5, 0.75)
    stiffness = centred(keys[8], (ELD, ELD), ELD ** -0.5, 0.3125)
    mass = centred(keys[9], (ELD, ELD), ELD ** -0.5, 0.3125)
    lifting = centred(keys[10], (ELD, NI), ELD ** -0.5, 0.3125)
    return dict(trace_rhs=trace_rhs, face_scale=face_scale, stiff_scale=stiff_scale, mass_scale=mass_scale, elem_faces=elem_faces, halo_faces=halo_faces, elem_count=elem_count, jacobi_block=jacobi_block, stiffness=stiffness, mass=mass, lifting=lifting)


def precondition(traces, face_scale, jacobi_block):
    row_count = traces.shape[0]
    flattened = traces.reshape(-1, FD)
    product = jnp.dot(flattened, jacobi_block, preferred_element_type=jnp.float32).reshape(row_count, -1)
    return (product * face_scale[:, None]).astype(jnp.bfloat16)


def global_faces(elem_faces, halo_faces):
    local_ids = elem_faces.reshape(PARTITIONS, E_DEV, 6)
    part_ids = jnp.arange(PARTITIONS, dtype=jnp.int32)[:, None, None]
    slot_ids = jnp.maximum(local_ids - F_DEV, 0)
    direction = (slot_ids // H).astype(jnp.int32)
    slot_pos = (slot_ids % H).astype(jnp.int32)
    opposite = (part_ids + PARTITIONS // 2) % PARTITIONS
    owner_part = jnp.where(direction == 0, part_ids - 2, jnp.where(direction == 1, part_ids + 2, opposite))
    owner_part = jnp.clip(owner_part, 0, PARTITIONS - 1).astype(jnp.int32)
    remote = owner_part * F_DEV + halo_faces[part_ids, direction, slot_pos]
    return jnp.where(local_ids < F_DEV, part_ids * F_DEV + local_ids, remote).astype(jnp.int32)


def apply_operator(traces, global_ids, elem_count, stiff_scale, mass_scale, stiffness, mass, lifting):
    src_count = traces.shape[1] // FD
    stiff_three = stiffness.astype(jnp.float32).reshape(6, FD, ELD)
    mass_three = mass.astype(jnp.float32).reshape(6, FD, ELD)
    lift_three = lifting.astype(jnp.float32).reshape(6, FD, NI)

    def scan_step(summed, pieces):
        part_gid, live_count, stiff_part, mass_part = pieces
        gathered = traces[part_gid.reshape(-1)].astype(jnp.float32).reshape(E_DEV, 6, src_count, FD)
        alive_mask = (jnp.arange(E_DEV) < live_count).astype(jnp.float32)
        stiff_term = jnp.einsum('efsd,fdk->esk', gathered, stiff_three)
        mass_term = jnp.einsum('efsd,fdk->esk', gathered, mass_three)
        terms = (stiff_part[:, None, None] * stiff_term - mass_part[:, None, None] * mass_term) * alive_mask[:, None, None]
        terms = terms.reshape(E_DEV, src_count, 6, FD).transpose(0, 2, 1, 3).reshape(E_DEV * 6, src_count * FD)
        summed = summed.at[part_gid.reshape(-1)].add(terms)
        interior_part = jnp.einsum('efsd,fdi->esi', gathered, lift_three) * alive_mask[:, None, None]
        interior_part = interior_part.astype(jnp.bfloat16).reshape(E_DEV, src_count * NI)
        return summed, interior_part

    start = jnp.zeros((FACES, traces.shape[1]), jnp.float32)
    summed, interior = lax.scan(scan_step, start, (global_ids, elem_count, stiff_scale.reshape(PARTITIONS, E_DEV), mass_scale.reshape(PARTITIONS, E_DEV)))
    return summed, interior.reshape(ELEMENTS, -1)


def reference(trace_rhs, face_scale, stiff_scale, mass_scale, elem_faces, halo_faces, elem_count, jacobi_block, stiffness, mass, lifting):
    global_ids = global_faces(elem_faces, halo_faces)
    first = precondition(trace_rhs, face_scale, jacobi_block)
    summed, unused = apply_operator(first, global_ids, elem_count, stiff_scale, mass_scale, stiffness, mass, lifting)
    second = precondition(summed.astype(jnp.bfloat16), face_scale, jacobi_block)
    applied, interior = apply_operator(second, global_ids, elem_count, stiff_scale, mass_scale, stiffness, mass, lifting)
    return applied.astype(jnp.bfloat16), interior
```

```python
import functools

import jax
import jax.numpy as jnp
from jax import lax
from jax.experimental import pallas as pl
from jax.experimental.pallas import tpu as pltpu
from jax.sharding import PartitionSpec as P

F32 = jnp.float32
BF16 = jnp.bfloat16
I32 = jnp.int32
LANES = 128
VMEM = pltpu.VMEM
SMEM = pltpu.SMEM


def iota(shape, dim):
    return lax.broadcasted_iota(I32, shape, dim)


def one_hot(condition):
    return jnp.where(condition, 1.0, 0.0).astype(BF16)


def matmul(a, b):
    return jnp.dot(a, b, preferred_element_type=F32)


def column_tiles(row):
    count = row.shape[1] // LANES
    return [
        jnp.transpose(
            jnp.broadcast_to(row[:, t * LANES : (t + 1) * LANES].astype(F32), (LANES, LANES))
        )
        for t in range(count)
    ]


def block_diagonal(block, copies):
    rows, cols = block.shape
    wide = jnp.concatenate([block] * copies, axis=1)
    full = jnp.concatenate([wide] * copies, axis=0)
    shape = (rows * copies, cols * copies)
    keep = (iota(shape, 0) // rows) == (iota(shape, 1) // cols)
    return jnp.where(keep, full, jnp.zeros_like(full))


def precondition(traces_ref, scale_ref, jacobi_ref, z_ref):
    rows, width = traces_ref.shape
    block = block_diagonal(jacobi_ref[...].astype(F32), 4).astype(BF16)
    scales = column_tiles(scale_ref[...])
    step = block.shape[0]
    for start in range(0, width, step):
        product = matmul(traces_ref[:, start : start + step], block)
        for t, scale in enumerate(scales):
            part = product[t * LANES : (t + 1) * LANES, :]
            both = jnp.concatenate([scale, scale], axis=1)
            z_ref[t * LANES : (t + 1) * LANES, start : start + step] = (part * both).astype(BF16)


def wanted_row(wanted_refs):
    row = jnp.concatenate([ref[...] for ref in wanted_refs], axis=1)
    pad = jnp.full((1, LANES - row.shape[1]), -1, I32)
    return jnp.concatenate([row, pad], axis=1)


def send_rows(wanted, z_ref, out_refs):
    faces = z_ref.shape[0]
    (column,) = column_tiles(wanted)
    column = column.astype(I32)
    lane = iota((LANES, LANES), 1)
    picks = jnp.concatenate(
        [one_hot(column == lane + t * LANES) for t in range(faces // LANES)], axis=1
    )
    rows = matmul(picks, z_ref[...]).astype(BF16)
    slots = out_refs[0].shape[0]
    for c, out_ref in enumerate(out_refs):
        out_ref[...] = rows[c * slots : (c + 1) * slots, :]


def first_kernel(rhs_ref, scale_ref, jacobi_ref, wa_ref, wb_ref, wc_ref, z_ref, *out_refs):
    precondition(rhs_ref, scale_ref, jacobi_ref, z_ref)
    send_rows(wanted_row([wa_ref, wb_ref, wc_ref]), z_ref, out_refs)


def paired_weight(src_ref, dst_ref, offset, face_dofs):
    rows, cols = src_ref.shape
    low = iota((face_dofs, LANES), 1) < face_dofs
    zero = jnp.zeros((face_dofs, LANES), F32)
    for k in range(rows // face_dofs):
        top = k * 2 * face_dofs
        for t in range(cols // LANES):
            tile = src_ref[k * face_dofs : (k + 1) * face_dofs, t * LANES : (t + 1) * LANES]
            tile = tile.astype(F32)
            turned = pltpu.roll(tile, face_dofs, 1)
            at = offset + 2 * t * LANES
            pieces = (
                (0, 0, jnp.where(low, tile, zero)),
                (1, 0, jnp.where(low, zero, turned)),
                (0, 1, jnp.where(low, turned, zero)),
                (1, 1, jnp.where(low, zero, tile)),
            )
            for half, odd, piece in pieces:
                dst_ref[
                    top + half * face_dofs : top + (half + 1) * face_dofs,
                    at + odd * LANES : at + (odd + 1) * LANES,
                ] = piece.astype(BF16)


def column_ids(par, faces, slots, tile, axis):
    index = iota((LANES, LANES), axis) + tile * LANES
    shift = slots * (1 - par)
    first = (index >= faces) & (index < faces + slots)
    second = (index >= faces + slots) & (index < faces + 2 * slots)
    return index + jnp.where(first, shift, 0) - jnp.where(second, shift, 0)


def gather_elements(faces_col, z_ref, arrived_refs, par, ext_ref, x_ref):
    faces, width = z_ref.shape
    slots = arrived_refs[0].shape[0]
    ext_ref[:faces, :] = z_ref[...]
    for c, ref in enumerate(arrived_refs):
        ext_ref[faces + c * slots : faces + (c + 1) * slots, :] = ref[...]
    filled = faces + 3 * slots
    ext_ref[filled:, :] = jnp.zeros((ext_ref.shape[0] - filled, width), BF16)
    tiles = ext_ref.shape[0] // LANES
    ids = [column_ids(par, faces, slots, t, 1) for t in range(tiles)]
    for k in range(6):
        mine = jnp.broadcast_to(faces_col[:, k : k + 1], (LANES, LANES))
        picks = jnp.concatenate([one_hot(mine == i) for i in ids], axis=1)
        rows = matmul(picks, ext_ref[...]).astype(BF16)
        for p in range(width // LANES):
            x_ref[p * LANES : (p + 1) * LANES, k * LANES : (k + 1) * LANES] = rows[
                :, p * LANES : (p + 1) * LANES
            ]


def element_terms(x_ref, w_ref, stiff_scale, mass_scale, y_ref):
    half = w_ref.shape[1] // 2
    stiff = jnp.concatenate([stiff_scale] * 6, axis=1)
    mass = jnp.concatenate([mass_scale] * 6, axis=1)
    rows = 2 * LANES
    for start in range(0, x_ref.shape[0], rows):
        product = matmul(x_ref[start : start + rows, :], w_ref[...])
        for r in range(rows // LANES):
            p = start // LANES + r
            part = product[r * LANES : (r + 1) * LANES, :]
            term = (stiff * part[:, :half] - mass * part[:, half:]).astype(BF16)
            for k in range(6):
                y_ref[k * LANES : (k + 1) * LANES, p * LANES : (p + 1) * LANES] = term[
                    :, k * LANES : (k + 1) * LANES
                ]


def scatter_elements(faces_col, par, y_ref, own_ref, back_refs, tiles):
    faces = own_ref.shape[0]
    slots = back_refs[0].shape[0]
    lane = iota((LANES, LANES), 1)
    spread = jnp.zeros((LANES, LANES), F32)
    for k in range(6):
        spread = jnp.where(lane == k, faces_col[:, k : k + 1].astype(F32), spread)
    turned = jnp.transpose(spread).astype(I32)
    order = list(range(faces // LANES, tiles)) + list(range(faces // LANES))
    for t in order:
        ids = column_ids(par, faces, slots, t, 0)
        picks = jnp.concatenate(
            [one_hot(ids == jnp.broadcast_to(turned[k : k + 1, :], (LANES, LANES))) for k in range(6)],
            axis=1,
        )
        rows = matmul(picks, y_ref[...])
        if t < faces // LANES:
            own_ref[t * LANES : (t + 1) * LANES, :] = rows
        else:
            for c, ref in enumerate(back_refs):
                ref[...] = rows[c * slots : (c + 1) * slots, :].astype(BF16)


def operator_kernel(
    with_interior,
    count_ref,
    par_ref,
    z_ref,
    aa_ref,
    ab_ref,
    ac_ref,
    faces_ref,
    stiff_scale_ref,
    mass_scale_ref,
    w_ref,
    *rest,
):
    if with_interior:
        lift_ref, own_ref, ba_ref, bb_ref, bc_ref, interior_ref, ext_ref, x_ref, y_ref = rest
    else:
        own_ref, ba_ref, bb_ref, bc_ref, ext_ref, x_ref, y_ref = rest
    par = par_ref[0]
    faces_col = faces_ref[...]
    alive = iota(faces_col.shape, 0) < count_ref[0]
    faces_col = jnp.where(alive, faces_col, -1)
    gather_elements(faces_col, z_ref, [aa_ref, ab_ref, ac_ref], par, ext_ref, x_ref)
    (stiff_scale,) = column_tiles(stiff_scale_ref[...])
    (mass_scale,) = column_tiles(mass_scale_ref[...])
    element_terms(x_ref, w_ref, stiff_scale, mass_scale, y_ref)
    scatter_elements(
        faces_col, par, y_ref, own_ref, [ba_ref, bb_ref, bc_ref], ext_ref.shape[0] // LANES
    )
    if with_interior:
        wide = lift_ref.shape[1]
        rows = 2 * LANES
        for start in range(0, x_ref.shape[0], rows):
            product = matmul(x_ref[start : start + rows, :], lift_ref[...]).astype(BF16)
            for r in range(rows // LANES):
                p = start // LANES + r
                interior_ref[:, p * wide : (p + 1) * wide] = product[
                    r * LANES : (r + 1) * LANES, :
                ]


def collect(own_ref, back_refs, wanted, gathered_ref):
    slots, width = back_refs[0].shape
    for c, ref in enumerate(back_refs):
        gathered_ref[c * slots : (c + 1) * slots, :] = ref[...]
    gathered_ref[3 * slots :, :] = jnp.zeros((LANES - 3 * slots, width), BF16)
    faces = own_ref.shape[0]
    target = jnp.broadcast_to(wanted, (faces, LANES))
    picks = one_hot(target == iota((faces, LANES), 0))
    return (own_ref[...] + matmul(picks, gathered_ref[...])).astype(BF16)


def middle_kernel(
    own_ref, ba_ref, bb_ref, bc_ref, wa_ref, wb_ref, wc_ref, scale_ref, jacobi_ref, z_ref,
    oa_ref, ob_ref, oc_ref, gathered_ref, v_ref
):
    wanted = wanted_row([wa_ref, wb_ref, wc_ref])
    v_ref[...] = collect(own_ref, [ba_ref, bb_ref, bc_ref], wanted, gathered_ref)
    precondition(v_ref, scale_ref, jacobi_ref, z_ref)
    send_rows(wanted, z_ref, [oa_ref, ob_ref, oc_ref])


def last_kernel(own_ref, ba_ref, bb_ref, bc_ref, wa_ref, wb_ref, wc_ref, out_ref, gathered_ref):
    wanted = wanted_row([wa_ref, wb_ref, wc_ref])
    out_ref[...] = collect(own_ref, [ba_ref, bb_ref, bc_ref], wanted, gathered_ref)


def weights_kernel(face_dofs, stiff_ref, mass_ref, lift_ref, w_ref, lift_out_ref):
    paired_weight(stiff_ref, w_ref, 0, face_dofs)
    paired_weight(mass_ref, w_ref, w_ref.shape[1] // 2, face_dofs)
    rows, inside = lift_ref.shape
    zero = jnp.zeros((face_dofs, inside), BF16)
    for k in range(rows // face_dofs):
        part = lift_ref[k * face_dofs : (k + 1) * face_dofs, :]
        top = 2 * k * face_dofs
        lift_out_ref[top : top + face_dofs, :inside] = part
        lift_out_ref[top : top + face_dofs, inside:] = zero
        lift_out_ref[top + face_dofs : top + 2 * face_dofs, :inside] = zero
        lift_out_ref[top + face_dofs : top + 2 * face_dofs, inside:] = part


def call(kernel, operands, scalars, outs, scratch, flops, name):
    specs = [pl.BlockSpec(memory_space=SMEM)] * len(scalars) + [
        pl.BlockSpec(memory_space=VMEM)
    ] * len(operands)
    moved = sum(a.size * a.dtype.itemsize for a in operands)
    return pl.pallas_call(
        kernel,
        out_shape=[jax.ShapeDtypeStruct(s, d) for s, d in outs],
        in_specs=specs,
        out_specs=[pl.BlockSpec(memory_space=VMEM)] * len(outs),
        scratch_shapes=[VMEM(s, d) for s, d in scratch],
        compiler_params=pltpu.CompilerParams(vmem_limit_bytes=32 * 1024 * 1024),
        cost_estimate=pl.CostEstimate(flops=flops, bytes_accessed=moved, transcendentals=0),
        name=name,
    )(*scalars, *operands)


def pairings(size):
    def both(pairs):
        return [pair for a, b in pairs for pair in ((a, b), (b, a))]

    even = both([(i, i + 1) for i in range(0, size - 1, 2)])
    odd = both([(i, i + 1) for i in range(1, size - 1, 2)])
    opposite = [(i, (i + size // 2) % size) for i in range(size)]
    return (even, odd, opposite)


def exchange(arrays, size):
    return [lax.ppermute(a, "elem", p) for a, p in zip(arrays, pairings(size))]


def per_device(
    size,
    trace_rhs,
    face_scale,
    stiff_scale,
    mass_scale,
    elem_faces,
    halo_faces,
    elem_count,
    jacobi_block,
    stiffness,
    mass,
    lifting,
):
    faces, width = trace_rhs.shape
    slots = halo_faces.shape[2]
    elems = elem_faces.shape[0]
    face_dofs = jacobi_block.shape[0]
    eld, inside = lifting.shape
    pairs = width // LANES
    ext_rows = -(-(faces + 3 * slots) // LANES) * LANES
    par = lax.axis_index("elem") % 2
    even = par == 0
    lists = [
        jnp.where(even, halo_faces[:, 1, :], halo_faces[:, 0, :]),
        jnp.where(even, halo_faces[:, 0, :], halo_faces[:, 1, :]),
        halo_faces[:, 2, :],
    ]
    par = par.astype(I32).reshape(1)
    wanted = exchange(lists, size)
    scale = face_scale.reshape(1, faces)
    stiff_row = stiff_scale.reshape(1, elems)
    mass_row = mass_scale.reshape(1, elems)
    paired, lift = call(
        functools.partial(weights_kernel, face_dofs),
        [stiffness, mass, lifting],
        [],
        [((2 * eld, 4 * eld), BF16), ((2 * eld, 2 * inside), BF16)],
        [],
        10_000_000,
        "weights",
    )
    field = ((faces, width), BF16)
    rows = [((slots, width), BF16)] * 3
    first, *outgoing = call(
        first_kernel,
        [trace_rhs, scale, jacobi_block, *wanted],
        [],
        [field, *rows],
        [],
        2 * faces * width * 256,
        "first",
    )
    arrived = exchange(outgoing, size)
    scratch = [
        ((ext_rows, width), BF16),
        ((pairs * elems, 6 * LANES), BF16),
        ((6 * elems, width), BF16),
    ]
    own_shape = ((faces, width), F32)
    own, *back = call(
        functools.partial(operator_kernel, False),
        [first, *arrived, elem_faces, stiff_row, mass_row, paired],
        [elem_count, par],
        [own_shape, *rows],
        scratch,
        4 * pairs * elems * 768 * 768,
        "operator",
    )
    returned = exchange(back, size)
    second, *outgoing = call(
        middle_kernel,
        [own, *returned, *wanted, scale, jacobi_block],
        [],
        [field, *rows],
        [((LANES, width), BF16), ((faces, width), BF16)],
        2 * faces * width * 256,
        "middle",
    )
    arrived = exchange(outgoing, size)
    own, b0, b1, b2, interior = call(
        functools.partial(operator_kernel, True),
        [second, *arrived, elem_faces, stiff_row, mass_row, paired, lift],
        [elem_count, par],
        [own_shape, *rows, ((elems, width // face_dofs * inside), BF16)],
        scratch,
        4 * pairs * elems * 768 * 768,
        "operator_interior",
    )
    returned = exchange([b0, b1, b2], size)
    (applied,) = call(
        last_kernel,
        [own, *returned, *wanted],
        [],
        [field],
        [((LANES, width), BF16)],
        2 * faces * width * 128,
        "last",
    )
    return (applied, interior)


def solution(mesh):
    rows = P(("grp", "elem", "sub"))
    split = P(("grp", "elem", "sub"), "src")
    in_specs = (
        split,
        rows,
        rows,
        rows,
        P(("grp", "elem", "sub"), None),
        P(("grp", "elem", "sub"), None, None),
        rows,
        P(),
        P(),
        P(),
        P(),
    )
    return jax.shard_map(
        functools.partial(per_device, mesh.shape["elem"]),
        mesh=mesh,
        in_specs=in_specs,
        out_specs=(split, split),
        check_vma=False,
    )
```

```python
import functools

import jax
import jax.numpy as jnp
from jax import lax
from jax.experimental import pallas as pl
from jax.experimental.pallas import tpu as pltpu
from jax.sharding import PartitionSpec as P

F32 = jnp.float32
BF16 = jnp.bfloat16
I32 = jnp.int32
LANES = 128
VMEM = pltpu.VMEM
SMEM = pltpu.SMEM
HBM = pltpu.HBM


def iota(shape, dim):
    return lax.broadcasted_iota(I32, shape, dim)


def one_hot(condition):
    return jnp.where(condition, 1.0, 0.0).astype(BF16)


def matmul(a, b):
    return jnp.dot(a, b, preferred_element_type=F32)


def column_tiles(row):
    count = row.shape[1] // LANES
    return [
        jnp.transpose(
            jnp.broadcast_to(row[:, t * LANES : (t + 1) * LANES].astype(F32), (LANES, LANES))
        )
        for t in range(count)
    ]


def block_diagonal(block, copies):
    rows, cols = block.shape
    wide = jnp.concatenate([block] * copies, axis=1)
    full = jnp.concatenate([wide] * copies, axis=0)
    shape = (rows * copies, cols * copies)
    keep = (iota(shape, 0) // rows) == (iota(shape, 1) // cols)
    return jnp.where(keep, full, jnp.zeros_like(full))


def precondition(traces_ref, scale_ref, jacobi_ref, z_ref):
    width = traces_ref.shape[1]
    block = block_diagonal(jacobi_ref[...].astype(F32), 4).astype(BF16)
    scales = column_tiles(scale_ref[...])
    step = block.shape[0]
    for start in range(0, width, step):
        product = matmul(traces_ref[:, start : start + step], block)
        for t, scale in enumerate(scales):
            part = product[t * LANES : (t + 1) * LANES, :]
            both = jnp.concatenate([scale, scale], axis=1)
            z_ref[t * LANES : (t + 1) * LANES, start : start + step] = (part * both).astype(BF16)


def paired_weight(src_ref, dst_ref, offset, face_dofs):
    rows, cols = src_ref.shape
    low = iota((face_dofs, LANES), 1) < face_dofs
    zero = jnp.zeros((face_dofs, LANES), F32)
    for k in range(rows // face_dofs):
        top = k * 2 * face_dofs
        for t in range(cols // LANES):
            tile = src_ref[k * face_dofs : (k + 1) * face_dofs, t * LANES : (t + 1) * LANES]
            tile = tile.astype(F32)
            turned = pltpu.roll(tile, face_dofs, 1)
            at = offset + 2 * t * LANES
            pieces = (
                (0, 0, jnp.where(low, tile, zero)),
                (1, 0, jnp.where(low, zero, turned)),
                (0, 1, jnp.where(low, turned, zero)),
                (1, 1, jnp.where(low, zero, tile)),
            )
            for half, odd, piece in pieces:
                dst_ref[
                    top + half * face_dofs : top + (half + 1) * face_dofs,
                    at + odd * LANES : at + (odd + 1) * LANES,
                ] = piece.astype(BF16)


def paired_lifting(src_ref, dst_ref, face_dofs):
    rows, inside = src_ref.shape
    zero = jnp.zeros((face_dofs, inside), BF16)
    for k in range(rows // face_dofs):
        part = src_ref[k * face_dofs : (k + 1) * face_dofs, :]
        top = 2 * k * face_dofs
        dst_ref[top : top + face_dofs, :inside] = part
        dst_ref[top : top + face_dofs, inside:] = zero
        dst_ref[top + face_dofs : top + 2 * face_dofs, :inside] = zero
        dst_ref[top + face_dofs : top + 2 * face_dofs, inside:] = part


def prepare_kernel(
    rhs_hbm, jacobi_hbm, stiff_hbm, mass_hbm, scale_hbm, z_ref, w_ref, scale_ref,
    rhs_ref, jacobi_ref, stiff_ref, mass_ref, line_ref, sems
):
    sources = (stiff_hbm, mass_hbm, jacobi_hbm, scale_hbm, rhs_hbm)
    targets = (stiff_ref, mass_ref, jacobi_ref, line_ref, rhs_ref)
    copies = [
        pltpu.make_async_copy(src, dst, sems.at[i])
        for i, (src, dst) in enumerate(zip(sources, targets))
    ]
    for copy in copies:
        copy.start()
    face_dofs = jacobi_ref.shape[0]
    copies[0].wait()
    paired_weight(stiff_ref, w_ref, 0, face_dofs)
    copies[1].wait()
    paired_weight(mass_ref, w_ref, w_ref.shape[1] // 2, face_dofs)
    copies[2].wait()
    copies[3].wait()
    scale_ref[...] = line_ref[...].reshape(scale_ref.shape)
    copies[4].wait()
    precondition(rhs_ref, scale_ref, jacobi_ref, z_ref)


def wanted_row(par, list_refs):
    picked = [jnp.where(par == 0, list_refs[0][0], list_refs[0][1])]
    picked.append(jnp.where(par == 0, list_refs[1][1], list_refs[1][0]))
    picked.append(list_refs[2][2])
    row = jnp.concatenate(picked, axis=1)
    pad = jnp.full((1, LANES - row.shape[1]), -1, I32)
    return jnp.concatenate([row, pad], axis=1)


def send_rows(wanted, z_ref, out_refs):
    faces = z_ref.shape[0]
    (column,) = column_tiles(wanted)
    column = column.astype(I32)
    lane = iota((LANES, LANES), 1)
    picks = jnp.concatenate(
        [one_hot(column == lane + t * LANES) for t in range(faces // LANES)], axis=1
    )
    rows = matmul(picks, z_ref[...]).astype(BF16)
    slots = out_refs[0].shape[0]
    for c, out_ref in enumerate(out_refs):
        out_ref[...] = rows[c * slots : (c + 1) * slots, :]


def send_kernel(par_ref, z_ref, la_ref, lb_ref, lc_ref, oa_ref, ob_ref, oc_ref, wanted_ref):
    wanted = wanted_row(par_ref[0], [la_ref, lb_ref, lc_ref])
    wanted_ref[...] = wanted
    send_rows(wanted, z_ref, [oa_ref, ob_ref, oc_ref])


def column_ids(par, faces, slots, tile, axis):
    index = iota((LANES, LANES), axis) + tile * LANES
    shift = slots * (1 - par)
    first = (index >= faces) & (index < faces + slots)
    second = (index >= faces + slots) & (index < faces + 2 * slots)
    return index + jnp.where(first, shift, 0) - jnp.where(second, shift, 0)


def tables_kernel(slots, faces, count_ref, par_ref, ids_ref, pick_ref, spread_ref):
    par = par_ref[0]
    ids_all = jnp.where(iota(ids_ref.shape, 1) < count_ref[0], ids_ref[...], -1)
    tiles = spread_ref.shape[0] // LANES
    lanes = [column_ids(par, faces, slots, t, 1) for t in range(tiles)]
    rows = [column_ids(par, faces, slots, t, 0) for t in range(tiles)]
    for k in range(ids_ref.shape[0]):
        across = jnp.broadcast_to(ids_all[k : k + 1, :], (LANES, LANES))
        down = jnp.transpose(across.astype(F32)).astype(I32)
        for t in range(tiles):
            pick_ref[k * LANES : (k + 1) * LANES, t * LANES : (t + 1) * LANES] = one_hot(
                down == lanes[t]
            )
            spread_ref[t * LANES : (t + 1) * LANES, k * LANES : (k + 1) * LANES] = one_hot(
                across == rows[t]
            )


def gather_kernel(pick_ref, z_ref, x_ref):
    faces, width = z_ref.shape
    for k in range(pick_ref.shape[0] // LANES):
        rows = matmul(pick_ref[k * LANES : (k + 1) * LANES, :faces], z_ref[...]).astype(BF16)
        for p in range(width // LANES):
            x_ref[p * LANES : (p + 1) * LANES, k * LANES : (k + 1) * LANES] = rows[
                :, p * LANES : (p + 1) * LANES
            ]


def operator_kernel(
    pick_ref, spread_ref, own_x_ref, aa_ref, ab_ref, ac_ref, stiff_scale_ref, mass_scale_ref,
    w_ref, y_ref, ba_ref, bb_ref, bc_ref, x_ref, halo_ref
):
    slots, width = aa_ref.shape
    for c, ref in enumerate((aa_ref, ab_ref, ac_ref)):
        halo_ref[c * slots : (c + 1) * slots, :] = ref[...]
    halo_ref[3 * slots :, :] = jnp.zeros((halo_ref.shape[0] - 3 * slots, width), BF16)
    faces = spread_ref.shape[0] - halo_ref.shape[0]
    for k in range(6):
        rows = matmul(pick_ref[k * LANES : (k + 1) * LANES, faces:], halo_ref[...]).astype(BF16)
        for p in range(width // LANES):
            at = (slice(p * LANES, (p + 1) * LANES), slice(k * LANES, (k + 1) * LANES))
            x_ref[at] = own_x_ref[at] + rows[:, p * LANES : (p + 1) * LANES]
    (stiff_scale,) = column_tiles(stiff_scale_ref[...])
    (mass_scale,) = column_tiles(mass_scale_ref[...])
    half = w_ref.shape[1] // 2
    stiff = jnp.concatenate([stiff_scale] * 6, axis=1)
    mass = jnp.concatenate([mass_scale] * 6, axis=1)
    step = 2 * LANES
    for start in range(0, x_ref.shape[0], step):
        product = matmul(x_ref[start : start + step, :], w_ref[...])
        for r in range(step // LANES):
            p = start // LANES + r
            part = product[r * LANES : (r + 1) * LANES, :]
            term = (stiff * part[:, :half] - mass * part[:, half:]).astype(BF16)
            for k in range(6):
                y_ref[k * LANES : (k + 1) * LANES, p * LANES : (p + 1) * LANES] = term[
                    :, k * LANES : (k + 1) * LANES
                ]
    rows = matmul(spread_ref[faces:, :], y_ref[...]).astype(BF16)
    for c, ref in enumerate((ba_ref, bb_ref, bc_ref)):
        ref[...] = rows[c * slots : (c + 1) * slots, :]


def own_sums(spread_ref, y_ref, own_ref):
    for t in range(own_ref.shape[0] // LANES):
        own_ref[t * LANES : (t + 1) * LANES, :] = matmul(
            spread_ref[t * LANES : (t + 1) * LANES, :], y_ref[...]
        )


def sums_kernel(spread_ref, y_ref, own_ref):
    own_sums(spread_ref, y_ref, own_ref)


def finish_kernel(
    face_dofs, spread_ref, y_ref, x_ref, lift_hbm, own_ref, interior_hbm,
    inside_ref, plain_ref, lift_ref, lift_sem, sems
):
    load = pltpu.make_async_copy(lift_hbm, plain_ref, lift_sem)
    load.start()
    own_sums(spread_ref, y_ref, own_ref)
    load.wait()
    paired_lifting(plain_ref, lift_ref, face_dofs)
    wide = lift_ref.shape[1]
    step = 2 * LANES
    copies = []
    for start in range(0, x_ref.shape[0], step):
        product = matmul(x_ref[start : start + step, :], lift_ref[...]).astype(BF16)
        first = start // LANES
        for r in range(step // LANES):
            inside_ref[:, (first + r) * wide : (first + r + 1) * wide] = product[
                r * LANES : (r + 1) * LANES, :
            ]
        span = pl.ds(first * wide, step // LANES * wide)
        copy = pltpu.make_async_copy(
            inside_ref.at[:, span], interior_hbm.at[:, span], sems.at[len(copies)]
        )
        copy.start()
        copies.append(copy)
    for copy in copies:
        copy.wait()


def collect(own_ref, back_refs, wanted, gathered_ref):
    slots, width = back_refs[0].shape
    for c, ref in enumerate(back_refs):
        gathered_ref[c * slots : (c + 1) * slots, :] = ref[...]
    gathered_ref[3 * slots :, :] = jnp.zeros((LANES - 3 * slots, width), BF16)
    faces = own_ref.shape[0]
    target = jnp.broadcast_to(wanted, (faces, LANES))
    picks = one_hot(target == iota((faces, LANES), 0))
    return (own_ref[...] + matmul(picks, gathered_ref[...])).astype(BF16)


def middle_kernel(
    own_ref, ba_ref, bb_ref, bc_ref, wanted_ref, scale_ref, jacobi_ref, z_ref,
    oa_ref, ob_ref, oc_ref, gathered_ref, v_ref
):
    wanted = wanted_ref[...]
    v_ref[...] = collect(own_ref, [ba_ref, bb_ref, bc_ref], wanted, gathered_ref)
    precondition(v_ref, scale_ref, jacobi_ref, z_ref)
    send_rows(wanted, z_ref, [oa_ref, ob_ref, oc_ref])


def last_kernel(own_ref, ba_ref, bb_ref, bc_ref, wanted_ref, out_ref, gathered_ref):
    out_ref[...] = collect(own_ref, [ba_ref, bb_ref, bc_ref], wanted_ref[...], gathered_ref)


def call(kernel, operands, spaces, outs, scratch, flops, name, out_spaces=None, grant=12):
    out_spaces = out_spaces or [VMEM] * len(outs)
    moved = sum(a.size * a.dtype.itemsize for a in operands)
    return pl.pallas_call(
        kernel,
        out_shape=[jax.ShapeDtypeStruct(s, d) for s, d in outs],
        in_specs=[pl.BlockSpec(memory_space=s) for s in spaces],
        out_specs=[pl.BlockSpec(memory_space=s) for s in out_spaces],
        scratch_shapes=scratch,
        compiler_params=pltpu.CompilerParams(vmem_limit_bytes=grant * 1024 * 1024),
        cost_estimate=pl.CostEstimate(flops=flops, bytes_accessed=moved, transcendentals=0),
        name=name,
    )(*operands)


def in_hbm(array):
    return pltpu.with_memory_space_constraint(array, HBM)


def pairings(size):
    def both(pairs):
        return [pair for a, b in pairs for pair in ((a, b), (b, a))]

    even = both([(i, i + 1) for i in range(0, size - 1, 2)])
    odd = both([(i, i + 1) for i in range(1, size - 1, 2)])
    opposite = [(i, (i + size // 2) % size) for i in range(size)]
    return (even, odd, opposite)


def exchange(arrays, size):
    return [lax.ppermute(a, "elem", p) for a, p in zip(arrays, pairings(size))]


def per_device(
    size,
    trace_rhs,
    face_scale,
    stiff_scale,
    mass_scale,
    elem_faces,
    halo_faces,
    elem_count,
    jacobi_block,
    stiffness,
    mass,
    lifting,
):
    faces, width = trace_rhs.shape
    slots = halo_faces.shape[2]
    elems = elem_faces.shape[0]
    face_dofs = jacobi_block.shape[0]
    eld, inside = lifting.shape
    pairs = width // LANES
    halo_rows = LANES
    ext_rows = faces + halo_rows
    slots_all = 6 * elems
    lists = exchange([halo_faces.transpose(1, 0, 2)] * 3, size)
    par = (lax.axis_index("elem") % 2).astype(I32).reshape(1)
    stiff_row = stiff_scale.reshape(1, elems)
    mass_row = mass_scale.reshape(1, elems)
    field = ((faces, width), BF16)
    rows = [((slots, width), BF16)] * 3
    x_shape = ((pairs * elems, 6 * LANES), BF16)
    y_shape = ((slots_all, width), BF16)
    own_shape = ((faces, width), F32)
    element_flops = 4 * pairs * elems * 768 * 768

    first, paired, scale = call(
        prepare_kernel,
        [in_hbm(a) for a in (trace_rhs, jacobi_block, stiffness, mass, face_scale)],
        [HBM] * 5,
        [field, ((2 * eld, 4 * eld), BF16), ((1, faces), F32)],
        [
            VMEM(trace_rhs.shape, BF16),
            VMEM(jacobi_block.shape, BF16),
            VMEM(stiffness.shape, BF16),
            VMEM(mass.shape, BF16),
            VMEM(face_scale.shape, F32),
            pltpu.SemaphoreType.DMA((5,)),
        ],
        2 * faces * width * 256,
        "prepare",
    )
    *outgoing, wanted = call(
        send_kernel,
        [par, first, *lists],
        [SMEM] + [VMEM] * 4,
        [*rows, ((1, LANES), I32)],
        [],
        2 * LANES * faces * width,
        "send",
    )
    arrived = exchange(outgoing, size)
    pick, spread = call(
        functools.partial(tables_kernel, slots, faces),
        [elem_count, par, elem_faces.T],
        [SMEM, SMEM, VMEM],
        [((slots_all, ext_rows), BF16), ((ext_rows, slots_all), BF16)],
        [],
        slots_all * ext_rows * 4,
        "tables",
    )

    def gather(z, name):
        (own_x,) = call(
            gather_kernel,
            [pick, z],
            [VMEM] * 2,
            [x_shape],
            [],
            2 * slots_all * faces * width,
            name,
        )
        return own_x

    def operator(own_x, arrived, keep_x, name):
        halo = VMEM((halo_rows, width), BF16)
        return call(
            operator_kernel,
            [pick, spread, own_x, *arrived, stiff_row, mass_row, paired],
            [VMEM] * 9,
            [y_shape, *rows] + ([x_shape] if keep_x else []),
            [halo] if keep_x else [VMEM(*x_shape), halo],
            element_flops,
            name,
        )

    own_x = gather(first, "gather1")
    y, *back = operator(own_x, arrived, False, "operator1")
    returned = exchange(back, size)
    (own,) = call(
        sums_kernel,
        [spread, y],
        [VMEM] * 2,
        [own_shape],
        [],
        2 * faces * slots_all * width,
        "sums1",
    )
    second, *outgoing = call(
        middle_kernel,
        [own, *returned, wanted, scale, jacobi_block],
        [VMEM] * 7,
        [field, *rows],
        [VMEM((LANES, width), BF16), VMEM((faces, width), BF16)],
        2 * faces * width * 256,
        "middle",
    )
    arrived = exchange(outgoing, size)
    own_x = gather(second, "gather2")
    y, *back, x = operator(own_x, arrived, True, "operator2")
    returned = exchange(back, size)
    own, interior = call(
        functools.partial(finish_kernel, face_dofs),
        [spread, y, x, in_hbm(lifting)],
        [VMEM] * 3 + [HBM],
        [own_shape, ((elems, width // face_dofs * inside), BF16)],
        [
            VMEM((elems, width // face_dofs * inside), BF16),
            VMEM(lifting.shape, BF16),
            VMEM((2 * eld, 2 * inside), BF16),
            pltpu.SemaphoreType.DMA,
            pltpu.SemaphoreType.DMA((pairs // 2,)),
        ],
        2 * pairs * elems * 768 * 1024,
        "finish",
        [VMEM, HBM],
    )
    (applied,) = call(
        last_kernel,
        [own, *returned, wanted],
        [VMEM] * 5,
        [field],
        [VMEM((LANES, width), BF16)],
        2 * faces * width * 128,
        "last",
    )
    return (applied, interior)


def solution(mesh):
    rows = P(("grp", "elem", "sub"))
    split = P(("grp", "elem", "sub"), "src")
    in_specs = (
        split,
        rows,
        rows,
        rows,
        P(("grp", "elem", "sub"), None),
        P(("grp", "elem", "sub"), None, None),
        rows,
        P(),
        P(),
        P(),
        P(),
    )
    return jax.shard_map(
        functools.partial(per_device, mesh.shape["elem"]),
        mesh=mesh,
        in_specs=in_specs,
        out_specs=(split, split),
        check_vma=False,
    )
```

```python
import functools

import jax
import jax.numpy as jnp
from jax import lax
from jax.experimental import pallas as pl
from jax.experimental.pallas import tpu as pltpu
from jax.sharding import PartitionSpec as P

F32 = jnp.float32
BF16 = jnp.bfloat16
I32 = jnp.int32
LANES = 128
VMEM = pltpu.VMEM
SMEM = pltpu.SMEM
HBM = pltpu.HBM


def iota(shape, dim):
    return lax.broadcasted_iota(I32, shape, dim)


def one_hot(condition):
    return jnp.where(condition, 1.0, 0.0).astype(BF16)


def matmul(a, b):
    return jnp.dot(a, b, preferred_element_type=F32)


def column_tiles(row):
    count = row.shape[1] // LANES
    return [
        jnp.transpose(
            jnp.broadcast_to(row[:, t * LANES : (t + 1) * LANES].astype(F32), (LANES, LANES))
        )
        for t in range(count)
    ]


def block_diagonal(block, copies):
    rows, cols = block.shape
    wide = jnp.concatenate([block] * copies, axis=1)
    full = jnp.concatenate([wide] * copies, axis=0)
    shape = (rows * copies, cols * copies)
    keep = (iota(shape, 0) // rows) == (iota(shape, 1) // cols)
    return jnp.where(keep, full, jnp.zeros_like(full))


def precondition(traces_ref, scale_ref, jacobi_ref, z_ref):
    width = traces_ref.shape[1]
    block = block_diagonal(jacobi_ref[...].astype(F32), 4).astype(BF16)
    scales = column_tiles(scale_ref[...])
    step = block.shape[0]
    for start in range(0, width, step):
        product = matmul(traces_ref[:, start : start + step], block)
        for t, scale in enumerate(scales):
            part = product[t * LANES : (t + 1) * LANES, :]
            both = jnp.concatenate([scale, scale], axis=1)
            z_ref[t * LANES : (t + 1) * LANES, start : start + step] = (part * both).astype(BF16)


def swap_halves(even, odd, low):
    turn = lambda tile: pltpu.roll(tile, LANES // 2, 1)
    return jnp.where(low, even, turn(odd)), jnp.where(low, turn(even), odd)


def prepare_kernel(
    rhs_hbm, jacobi_hbm, stiff_hbm, mass_hbm, scale_hbm, z_ref, w_ref, scale_ref,
    rhs_ref, jacobi_ref, line_ref, sems
):
    half = w_ref.shape[1] // 2
    sources = (jacobi_hbm, scale_hbm, rhs_hbm, stiff_hbm, mass_hbm)
    targets = (jacobi_ref, line_ref, rhs_ref, w_ref.at[:, :half], w_ref.at[:, half:])
    copies = [
        pltpu.make_async_copy(src, dst, sems.at[i])
        for i, (src, dst) in enumerate(zip(sources, targets))
    ]
    for copy in copies:
        copy.start()
    copies[0].wait()
    copies[1].wait()
    scale_ref[...] = line_ref[...].reshape(scale_ref.shape)
    copies[2].wait()
    precondition(rhs_ref, scale_ref, jacobi_ref, z_ref)
    copies[3].wait()
    copies[4].wait()


def wanted_part(par, list_ref, colour):
    if colour == 2:
        return list_ref[2]
    return jnp.where(par == colour, list_ref[0], list_ref[1])


def padded(row):
    return jnp.concatenate([row, jnp.full((1, LANES - row.shape[1]), -1, I32)], axis=1)


def wanted_row(par, list_refs):
    parts = [wanted_part(par, ref, c) for c, ref in enumerate(list_refs)]
    return padded(jnp.concatenate(parts, axis=1))


def picked_rows(wanted, z_ref, count):
    (column,) = column_tiles(wanted)
    column = column[:count].astype(I32)
    lane = iota((count, LANES), 1)
    picks = jnp.concatenate(
        [one_hot(column == lane + t * LANES) for t in range(z_ref.shape[0] // LANES)], axis=1
    )
    return matmul(picks, z_ref[...]).astype(BF16)


def send_kernel(colour, par_ref, z_ref, list_ref, *refs):
    out_ref = refs[-1]
    wanted = padded(wanted_part(par_ref[0], list_ref, colour))
    out_ref[...] = picked_rows(wanted, z_ref, out_ref.shape[0])


def column_ids(par, faces, slots, tile, axis):
    index = iota((LANES, LANES), axis) + tile * LANES
    shift = slots * (1 - par)
    first = (index >= faces) & (index < faces + slots)
    second = (index >= faces + slots) & (index < faces + 2 * slots)
    return index + jnp.where(first, shift, 0) - jnp.where(second, shift, 0)


def tables_kernel(slots, faces, count_ref, par_ref, ids_ref, own_ref, halo_ref, spread_ref):
    par = par_ref[0]
    ids_all = jnp.where(iota(ids_ref.shape, 1) < count_ref[0], ids_ref[...], -1)
    tiles = spread_ref.shape[0] // LANES
    owned = faces // LANES
    lanes = [column_ids(par, faces, slots, t, 1) for t in range(tiles)]
    rows = [column_ids(par, faces, slots, t, 0) for t in range(tiles)]
    span = lambda i: slice(i * LANES, (i + 1) * LANES)
    for k in range(ids_ref.shape[0]):
        across = jnp.broadcast_to(ids_all[k : k + 1, :], (LANES, LANES))
        down = jnp.transpose(across.astype(F32)).astype(I32)
        for t in range(tiles):
            pick = one_hot(down == lanes[t])
            if t < owned:
                own_ref[span(k), span(t)] = pick
            else:
                halo_ref[span(k // 2), span(k % 2)] = pick
            spread_ref[span(t), span(k)] = one_hot(across == rows[t])


def gather_kernel(pick_ref, z_ref, x_ref):
    width = z_ref.shape[1]
    low = iota((LANES, LANES), 1) < LANES // 2
    for t in range(x_ref.shape[1] // LANES):
        rows = matmul(pick_ref[2 * t * LANES : 2 * (t + 1) * LANES, :], z_ref[...])
        for p in range(width // LANES):
            pair = rows[:, p * LANES : (p + 1) * LANES]
            even, odd = swap_halves(pair[:LANES], pair[LANES:], low)
            at = 2 * p * LANES
            x_ref[at : at + LANES, t * LANES : (t + 1) * LANES] = even.astype(BF16)
            x_ref[at + LANES : at + 2 * LANES, t * LANES : (t + 1) * LANES] = odd.astype(BF16)


def operator_kernel(
    pick_ref, spread_ref, own_x_ref, aa_ref, ab_ref, ac_ref, stiff_scale_ref, mass_scale_ref,
    w_ref, y_ref, ba_ref, bb_ref, bc_ref, x_ref, halo_ref
):
    slots, width = aa_ref.shape
    pairs = width // LANES
    filled = 3 * slots
    arrived = jnp.concatenate([aa_ref[...], ab_ref[...], ac_ref[...]], axis=0).astype(F32)
    low = iota((filled, LANES), 1) < LANES // 2
    zero = jnp.zeros((filled, LANES), F32)
    for first in (0, LANES):
        halo_ref[first + filled : first + LANES, :] = jnp.zeros(
            (LANES - filled, halo_ref.shape[1]), BF16
        )
    for p in range(pairs):
        tile = arrived[:, p * LANES : (p + 1) * LANES]
        turned = pltpu.roll(tile, LANES // 2, 1)
        even = slice(2 * p * LANES, (2 * p + 1) * LANES)
        odd = slice((2 * p + 1) * LANES, (2 * p + 2) * LANES)
        halo_ref[:filled, even] = jnp.where(low, tile, zero).astype(BF16)
        halo_ref[LANES : LANES + filled, even] = jnp.where(low, zero, turned).astype(BF16)
        halo_ref[:filled, odd] = jnp.where(low, turned, zero).astype(BF16)
        halo_ref[LANES : LANES + filled, odd] = jnp.where(low, zero, tile).astype(BF16)
    for t in range(x_ref.shape[1] // LANES):
        rows = matmul(pick_ref[t * LANES : (t + 1) * LANES, :], halo_ref[...]).astype(BF16)
        for s in range(2 * pairs):
            at = (slice(s * LANES, (s + 1) * LANES), slice(t * LANES, (t + 1) * LANES))
            x_ref[at] = own_x_ref[at] + rows[:, s * LANES : (s + 1) * LANES]
    (stiff_scale,) = column_tiles(stiff_scale_ref[...])
    (mass_scale,) = column_tiles(mass_scale_ref[...])
    stiff = jnp.concatenate([stiff_scale] * 2, axis=0)
    mass = jnp.concatenate([mass_scale] * 2, axis=0)
    low = iota((LANES, LANES), 1) < LANES // 2
    half = w_ref.shape[1] // 2
    for p in range(pairs):
        product = matmul(x_ref[2 * p * LANES : 2 * (p + 1) * LANES, :], w_ref[...])
        for t in range(half // LANES):
            at = t * LANES
            term = (
                stiff * product[:, at : at + LANES]
                - mass * product[:, half + at : half + at + LANES]
            )
            first, second = swap_halves(term[:LANES], term[LANES:], low)
            place = slice(p * LANES, (p + 1) * LANES)
            y_ref[2 * at : 2 * at + LANES, place] = first.astype(BF16)
            y_ref[2 * at + LANES : 2 * at + 2 * LANES, place] = second.astype(BF16)
    rows = matmul(spread_ref[spread_ref.shape[0] - LANES :, :], y_ref[...]).astype(BF16)
    for c, ref in enumerate((ba_ref, bb_ref, bc_ref)):
        ref[...] = rows[c * slots : (c + 1) * slots, :]


def own_sums(spread_ref, y_ref, own_ref):
    for t in range(own_ref.shape[0] // LANES):
        own_ref[t * LANES : (t + 1) * LANES, :] = matmul(
            spread_ref[t * LANES : (t + 1) * LANES, :], y_ref[...]
        )


def sums_kernel(spread_ref, y_ref, own_ref):
    own_sums(spread_ref, y_ref, own_ref)


def finish_kernel(
    spread_ref, y_ref, x_ref, lift_hbm, own_ref, interior_hbm, inside_ref, lift_ref, lift_sem, sems
):
    load = pltpu.make_async_copy(lift_hbm, lift_ref, lift_sem)
    load.start()
    own_sums(spread_ref, y_ref, own_ref)
    load.wait()
    wide = lift_ref.shape[1]
    step = 4
    copies = []
    for start in range(0, x_ref.shape[0] // LANES, step):
        rows = x_ref[start * LANES : (start + step) * LANES, :]
        product = matmul(rows, lift_ref[...]).astype(BF16)
        for r in range(step):
            inside_ref[:, (start + r) * wide : (start + r + 1) * wide] = product[
                r * LANES : (r + 1) * LANES, :
            ]
        span = pl.ds(start * wide, step * wide)
        copy = pltpu.make_async_copy(
            inside_ref.at[:, span], interior_hbm.at[:, span], sems.at[len(copies)]
        )
        copy.start()
        copies.append(copy)
    for copy in copies:
        copy.wait()


def gather_back(back_refs, gathered_ref):
    slots, width = back_refs[0].shape
    for c, ref in enumerate(back_refs):
        gathered_ref[c * slots : (c + 1) * slots, :] = ref[...]
    gathered_ref[3 * slots :, :] = jnp.zeros((LANES - 3 * slots, width), BF16)


def collected(own_ref, wanted, gathered_ref, tile):
    target = jnp.broadcast_to(wanted, (LANES, LANES))
    picks = one_hot(target == iota((LANES, LANES), 0) + tile * LANES)
    own = own_ref[tile * LANES : (tile + 1) * LANES, :]
    return (own + matmul(picks, gathered_ref[...])).astype(BF16)


def middle_kernel(
    par_ref, own_ref, ba_ref, bb_ref, bc_ref, la_ref, lb_ref, lc_ref, scale_ref, jacobi_ref, z_ref,
    oa_ref, ob_ref, oc_ref, gathered_ref, v_ref
):
    wanted = wanted_row(par_ref[0], [la_ref, lb_ref, lc_ref])
    gather_back([ba_ref, bb_ref, bc_ref], gathered_ref)
    for t in range(own_ref.shape[0] // LANES):
        v_ref[t * LANES : (t + 1) * LANES, :] = collected(own_ref, wanted, gathered_ref, t)
    precondition(v_ref, scale_ref, jacobi_ref, z_ref)
    rows = picked_rows(wanted, z_ref, LANES)
    slots = oa_ref.shape[0]
    for c, ref in enumerate((oa_ref, ob_ref, oc_ref)):
        ref[...] = rows[c * slots : (c + 1) * slots, :]


def last_kernel(
    par_ref, own_ref, ba_ref, bb_ref, bc_ref, la_ref, lb_ref, lc_ref, out_hbm, gathered_ref,
    out_ref, sems
):
    wanted = wanted_row(par_ref[0], [la_ref, lb_ref, lc_ref])
    gather_back([ba_ref, bb_ref, bc_ref], gathered_ref)
    copies = []
    for t in range(own_ref.shape[0] // LANES):
        span = pl.ds(t * LANES, LANES)
        out_ref[span, :] = collected(own_ref, wanted, gathered_ref, t)
        copy = pltpu.make_async_copy(out_ref.at[span, :], out_hbm.at[span, :], sems.at[t])
        copy.start()
        copies.append(copy)
    for copy in copies:
        copy.wait()


def call(kernel, operands, spaces, outs, scratch, flops, name, out_spaces=None, grant=12):
    out_spaces = out_spaces or [VMEM] * len(outs)
    moved = sum(a.size * a.dtype.itemsize for a in operands)
    return pl.pallas_call(
        kernel,
        out_shape=[jax.ShapeDtypeStruct(s, d) for s, d in outs],
        in_specs=[pl.BlockSpec(memory_space=s) for s in spaces],
        out_specs=[pl.BlockSpec(memory_space=s) for s in out_spaces],
        scratch_shapes=scratch,
        compiler_params=pltpu.CompilerParams(vmem_limit_bytes=grant * 1024 * 1024),
        cost_estimate=pl.CostEstimate(flops=flops, bytes_accessed=moved, transcendentals=0),
        name=name,
    )(*operands)


def in_hbm(array):
    return pltpu.with_memory_space_constraint(array, HBM)


def pairings(size):
    def both(pairs):
        return [pair for a, b in pairs for pair in ((a, b), (b, a))]

    even = both([(i, i + 1) for i in range(0, size - 1, 2)])
    odd = both([(i, i + 1) for i in range(1, size - 1, 2)])
    opposite = [(i, (i + size // 2) % size) for i in range(size)]
    return (even, odd, opposite)


def exchange(arrays, size):
    ways = pairings(size)
    got = {c: lax.ppermute(arrays[c], "elem", ways[c]) for c in (2, 1, 0)}
    return [got[c] for c in range(3)]


def per_device(
    size,
    trace_rhs,
    face_scale,
    stiff_scale,
    mass_scale,
    elem_faces,
    halo_faces,
    elem_count,
    jacobi_block,
    stiffness,
    mass,
    lifting,
):
    faces, width = trace_rhs.shape
    slots = halo_faces.shape[2]
    elems = elem_faces.shape[0]
    face_dofs = jacobi_block.shape[0]
    eld, inside = lifting.shape
    pairs = width // LANES
    halo_rows = LANES
    ext_rows = faces + halo_rows
    slots_all = 6 * elems
    lists = exchange([halo_faces.transpose(1, 0, 2)] * 3, size)
    par = (lax.axis_index("elem") % 2).astype(I32).reshape(1)
    stiff_row = stiff_scale.reshape(1, elems)
    mass_row = mass_scale.reshape(1, elems)
    field = ((faces, width), BF16)
    rows = [((slots, width), BF16)] * 3
    x_shape = ((2 * pairs * elems, eld), BF16)
    y_shape = ((slots_all, width), BF16)
    own_shape = ((faces, width), F32)
    element_flops = 4 * 2 * pairs * elems * eld * eld

    first, weights, scale = call(
        prepare_kernel,
        [in_hbm(a) for a in (trace_rhs, jacobi_block, stiffness, mass, face_scale)],
        [HBM] * 5,
        [field, ((eld, 2 * eld), BF16), ((1, faces), F32)],
        [
            VMEM(trace_rhs.shape, BF16),
            VMEM(jacobi_block.shape, BF16),
            VMEM(face_scale.shape, F32),
            pltpu.SemaphoreType.DMA((5,)),
        ],
        2 * faces * width * 256,
        "prepare",
    )
    outgoing = [None] * 3
    before = []
    for c in (2, 1, 0):
        (outgoing[c],) = call(
            functools.partial(send_kernel, c),
            [par, first, lists[c], *before],
            [SMEM] + [VMEM] * 2 + [pl.ANY] * len(before),
            rows[:1],
            [],
            2 * LANES * faces * width,
            f"send{c}",
        )
        before = [outgoing[c]]
    arrived = exchange(outgoing, size)
    own_pick, halo_pick, spread = call(
        functools.partial(tables_kernel, slots, faces),
        [elem_count, par, elem_faces.T],
        [SMEM, SMEM, VMEM],
        [
            ((slots_all, faces), BF16),
            ((slots_all // 2, 2 * halo_rows), BF16),
            ((ext_rows, slots_all), BF16),
        ],
        [],
        slots_all * ext_rows * 4,
        "tables",
    )

    def gather(z, name):
        (own_x,) = call(
            gather_kernel,
            [own_pick, z],
            [VMEM] * 2,
            [x_shape],
            [],
            2 * slots_all * faces * width,
            name,
        )
        return own_x

    def operator(own_x, arrived, keep_x, name):
        halo = VMEM((2 * halo_rows, 2 * width), BF16)
        return call(
            operator_kernel,
            [halo_pick, spread, own_x, *arrived, stiff_row, mass_row, weights],
            [VMEM] * 9,
            [y_shape, *rows] + ([x_shape] if keep_x else []),
            [halo] if keep_x else [VMEM(*x_shape), halo],
            element_flops,
            name,
        )

    own_x = gather(first, "gather1")
    y, *back = operator(own_x, arrived, False, "operator1")
    returned = exchange(back, size)
    (own,) = call(
        sums_kernel,
        [spread, y],
        [VMEM] * 2,
        [own_shape],
        [],
        2 * faces * slots_all * width,
        "sums1",
    )
    second, *outgoing = call(
        middle_kernel,
        [par, own, *returned, *lists, scale, jacobi_block],
        [SMEM] + [VMEM] * 9,
        [field, *rows],
        [VMEM((LANES, width), BF16), VMEM((faces, width), BF16)],
        2 * faces * width * 256,
        "middle",
    )
    arrived = exchange(outgoing, size)
    own_x = gather(second, "gather2")
    y, *back, x = operator(own_x, arrived, True, "operator2")
    returned = exchange(back, size)
    own, interior = call(
        finish_kernel,
        [spread, y, x, in_hbm(lifting)],
        [VMEM] * 3 + [HBM],
        [own_shape, ((elems, width // face_dofs * inside), BF16)],
        [
            VMEM((elems, width // face_dofs * inside), BF16),
            VMEM(lifting.shape, BF16),
            pltpu.SemaphoreType.DMA,
            pltpu.SemaphoreType.DMA((pairs // 2,)),
        ],
        4 * pairs * elems * eld * inside,
        "finish",
        [VMEM, HBM],
    )
    (applied,) = call(
        last_kernel,
        [par, own, *returned, *lists],
        [SMEM] + [VMEM] * 7,
        [field],
        [
            VMEM((LANES, width), BF16),
            VMEM((faces, width), BF16),
            pltpu.SemaphoreType.DMA((faces // LANES,)),
        ],
        2 * faces * width * 128,
        "last",
        [HBM],
    )
    return (applied, interior)


def solution(mesh):
    rows = P(("grp", "elem", "sub"))
    split = P(("grp", "elem", "sub"), "src")
    in_specs = (
        split,
        rows,
        rows,
        rows,
        P(("grp", "elem", "sub"), None),
        P(("grp", "elem", "sub"), None, None),
        rows,
        P(),
        P(),
        P(),
        P(),
    )
    return jax.shard_map(
        functools.partial(per_device, mesh.shape["elem"]),
        mesh=mesh,
        in_specs=in_specs,
        out_specs=(split, split),
        check_vma=False,
    )
```

```python
import functools

import jax
import jax.numpy as jnp
from jax import lax
from jax.experimental import pallas as pl
from jax.experimental.pallas import tpu as pltpu
from jax.sharding import PartitionSpec as P

F32 = jnp.float32
BF16 = jnp.bfloat16
I32 = jnp.int32
LANES = 128
VMEM = pltpu.VMEM
SMEM = pltpu.SMEM
HBM = pltpu.HBM


def iota(shape, dim):
    return lax.broadcasted_iota(I32, shape, dim)


def one_hot(condition):
    return jnp.where(condition, 1.0, 0.0).astype(BF16)


def matmul(a, b):
    return jnp.dot(a, b, preferred_element_type=F32)


def column_tiles(row):
    count = row.shape[1] // LANES
    return [
        jnp.transpose(
            jnp.broadcast_to(row[:, t * LANES : (t + 1) * LANES].astype(F32), (LANES, LANES))
        )
        for t in range(count)
    ]


def block_diagonal(block, copies):
    rows, cols = block.shape
    wide = jnp.concatenate([block] * copies, axis=1)
    full = jnp.concatenate([wide] * copies, axis=0)
    shape = (rows * copies, cols * copies)
    keep = (iota(shape, 0) // rows) == (iota(shape, 1) // cols)
    return jnp.where(keep, full, jnp.zeros_like(full))


def precondition(traces_ref, scale_ref, jacobi_ref, z_ref):
    width = traces_ref.shape[1]
    block = block_diagonal(jacobi_ref[...].astype(F32), 4).astype(BF16)
    scales = column_tiles(scale_ref[...])
    step = block.shape[0]
    for start in range(0, width, step):
        product = matmul(traces_ref[:, start : start + step], block)
        for t, scale in enumerate(scales):
            part = product[t * LANES : (t + 1) * LANES, :]
            both = jnp.concatenate([scale, scale], axis=1)
            z_ref[t * LANES : (t + 1) * LANES, start : start + step] = (part * both).astype(BF16)


def swap_halves(even, odd, low):
    turn = lambda tile: pltpu.roll(tile, LANES // 2, 1)
    return jnp.where(low, even, turn(odd)), jnp.where(low, turn(even), odd)


def prepare_kernel(
    rhs_hbm, jacobi_hbm, stiff_hbm, mass_hbm, scale_hbm, z_ref, w_ref, scale_ref,
    rhs_ref, jacobi_ref, line_ref, sems
):
    half = w_ref.shape[1] // 2
    sources = (jacobi_hbm, scale_hbm, rhs_hbm, stiff_hbm, mass_hbm)
    targets = (jacobi_ref, line_ref, rhs_ref, w_ref.at[:, :half], w_ref.at[:, half:])
    copies = [
        pltpu.make_async_copy(src, dst, sems.at[i])
        for i, (src, dst) in enumerate(zip(sources, targets))
    ]
    for copy in copies:
        copy.start()
    copies[0].wait()
    copies[1].wait()
    scale_ref[...] = line_ref[...].reshape(scale_ref.shape)
    copies[2].wait()
    precondition(rhs_ref, scale_ref, jacobi_ref, z_ref)
    copies[3].wait()
    copies[4].wait()


def wanted_part(par, list_ref, colour):
    if colour == 0:
        return list_ref[2]
    return jnp.where(par == 2 - colour, list_ref[0], list_ref[1])


def padded(row):
    return jnp.concatenate([row, jnp.full((1, LANES - row.shape[1]), -1, I32)], axis=1)


def wanted_row(par, list_refs):
    parts = [wanted_part(par, ref, c) for c, ref in enumerate(list_refs)]
    return padded(jnp.concatenate(parts, axis=1))


def send_rows(wanted, z_ref, out_refs):
    (column,) = column_tiles(wanted)
    column = column.astype(I32)
    lane = iota((LANES, LANES), 1)
    picks = jnp.concatenate(
        [one_hot(column == lane + t * LANES) for t in range(z_ref.shape[0] // LANES)], axis=1
    )
    rows = matmul(picks, z_ref[...]).astype(BF16)
    slots = out_refs[0].shape[0]
    for c, ref in enumerate(out_refs):
        ref[...] = rows[c * slots : (c + 1) * slots, :]


def send_kernel(par_ref, z_ref, la_ref, lb_ref, lc_ref, *out_refs):
    send_rows(wanted_row(par_ref[0], [la_ref, lb_ref, lc_ref]), z_ref, out_refs)


def column_ids(par, faces, slots, tile, axis):
    index = iota((LANES, LANES), axis) + tile * LANES
    moved = jnp.where(index < faces + slots, 2 * slots, slots * par - slots)
    moved = jnp.where(index < faces + 2 * slots, moved, -slots - slots * par)
    return jnp.where(index < faces, index, index + moved)


def tables_kernel(slots, faces, count_ref, par_ref, ids_ref, own_ref, halo_ref, spread_ref):
    par = par_ref[0]
    ids_all = jnp.where(iota(ids_ref.shape, 1) < count_ref[0], ids_ref[...], -1)
    tiles = spread_ref.shape[0] // LANES
    owned = faces // LANES
    lanes = [column_ids(par, faces, slots, t, 1) for t in range(tiles)]
    rows = [column_ids(par, faces, slots, t, 0) for t in range(tiles)]
    span = lambda i: slice(i * LANES, (i + 1) * LANES)
    for k in range(ids_ref.shape[0]):
        across = jnp.broadcast_to(ids_all[k : k + 1, :], (LANES, LANES))
        down = jnp.transpose(across.astype(F32)).astype(I32)
        for t in range(tiles):
            pick = one_hot(down == lanes[t])
            if t < owned:
                own_ref[span(k), span(t)] = pick
            else:
                halo_ref[span(k // 2), span(k % 2)] = pick
            spread_ref[span(t), span(k)] = one_hot(across == rows[t])


def gather_lift_kernel(pick_ref, z_ref, lift_hbm, x_ref, lift_ref, sem):
    load = pltpu.make_async_copy(lift_hbm, lift_ref, sem)
    load.start()
    gather_kernel(pick_ref, z_ref, x_ref)
    load.wait()


def gather_kernel(pick_ref, z_ref, x_ref):
    width = z_ref.shape[1]
    low = iota((LANES, LANES), 1) < LANES // 2
    for t in range(x_ref.shape[1] // LANES):
        rows = matmul(pick_ref[2 * t * LANES : 2 * (t + 1) * LANES, :], z_ref[...])
        for p in range(width // LANES):
            pair = rows[:, p * LANES : (p + 1) * LANES]
            even, odd = swap_halves(pair[:LANES], pair[LANES:], low)
            at = 2 * p * LANES
            x_ref[at : at + LANES, t * LANES : (t + 1) * LANES] = even.astype(BF16)
            x_ref[at + LANES : at + 2 * LANES, t * LANES : (t + 1) * LANES] = odd.astype(BF16)


def operator_kernel(
    pick_ref, spread_ref, own_x_ref, aa_ref, ab_ref, ac_ref, stiff_scale_ref, mass_scale_ref,
    w_ref, y_ref, ba_ref, bb_ref, bc_ref, x_ref, halo_ref
):
    slots, width = aa_ref.shape
    pairs = width // LANES
    filled = 3 * slots
    arrived = jnp.concatenate([aa_ref[...], ab_ref[...], ac_ref[...]], axis=0).astype(F32)
    low = iota((filled, LANES), 1) < LANES // 2
    zero = jnp.zeros((filled, LANES), F32)
    for first in (0, LANES):
        halo_ref[first + filled : first + LANES, :] = jnp.zeros(
            (LANES - filled, halo_ref.shape[1]), BF16
        )
    for p in range(pairs):
        tile = arrived[:, p * LANES : (p + 1) * LANES]
        turned = pltpu.roll(tile, LANES // 2, 1)
        even = slice(2 * p * LANES, (2 * p + 1) * LANES)
        odd = slice((2 * p + 1) * LANES, (2 * p + 2) * LANES)
        halo_ref[:filled, even] = jnp.where(low, tile, zero).astype(BF16)
        halo_ref[LANES : LANES + filled, even] = jnp.where(low, zero, turned).astype(BF16)
        halo_ref[:filled, odd] = jnp.where(low, turned, zero).astype(BF16)
        halo_ref[LANES : LANES + filled, odd] = jnp.where(low, zero, tile).astype(BF16)
    for t in range(x_ref.shape[1] // LANES):
        rows = matmul(pick_ref[t * LANES : (t + 1) * LANES, :], halo_ref[...]).astype(BF16)
        for s in range(2 * pairs):
            at = (slice(s * LANES, (s + 1) * LANES), slice(t * LANES, (t + 1) * LANES))
            x_ref[at] = own_x_ref[at] + rows[:, s * LANES : (s + 1) * LANES]
    (stiff_scale,) = column_tiles(stiff_scale_ref[...])
    (mass_scale,) = column_tiles(mass_scale_ref[...])
    stiff = jnp.concatenate([stiff_scale] * 2, axis=0)
    mass = jnp.concatenate([mass_scale] * 2, axis=0)
    low = iota((LANES, LANES), 1) < LANES // 2
    half = w_ref.shape[1] // 2
    for p in range(pairs):
        product = matmul(x_ref[2 * p * LANES : 2 * (p + 1) * LANES, :], w_ref[...])
        for t in range(half // LANES):
            at = t * LANES
            term = (
                stiff * product[:, at : at + LANES]
                - mass * product[:, half + at : half + at + LANES]
            )
            first, second = swap_halves(term[:LANES], term[LANES:], low)
            place = slice(p * LANES, (p + 1) * LANES)
            y_ref[2 * at : 2 * at + LANES, place] = first.astype(BF16)
            y_ref[2 * at + LANES : 2 * at + 2 * LANES, place] = second.astype(BF16)
    rows = matmul(spread_ref[spread_ref.shape[0] - LANES :, :], y_ref[...]).astype(BF16)
    for c, ref in enumerate((ba_ref, bb_ref, bc_ref)):
        ref[...] = rows[c * slots : (c + 1) * slots, :]


def own_sums(spread_ref, y_ref, own_ref):
    for t in range(own_ref.shape[0] // LANES):
        own_ref[t * LANES : (t + 1) * LANES, :] = matmul(
            spread_ref[t * LANES : (t + 1) * LANES, :], y_ref[...]
        )


def sums_kernel(spread_ref, y_ref, own_ref):
    own_sums(spread_ref, y_ref, own_ref)


def finish_kernel(
    spread_ref, y_ref, x_ref, lift_ref, own_ref, interior_hbm, inside_ref, sems
):
    wide = lift_ref.shape[1]
    step = 4
    copies = []
    for start in range(0, x_ref.shape[0] // LANES, step):
        rows = x_ref[start * LANES : (start + step) * LANES, :]
        product = matmul(rows, lift_ref[...]).astype(BF16)
        for r in range(step):
            inside_ref[:, (start + r) * wide : (start + r + 1) * wide] = product[
                r * LANES : (r + 1) * LANES, :
            ]
        span = pl.ds(start * wide, step * wide)
        copy = pltpu.make_async_copy(
            inside_ref.at[:, span], interior_hbm.at[:, span], sems.at[len(copies)]
        )
        copy.start()
        copies.append(copy)
    own_sums(spread_ref, y_ref, own_ref)
    for copy in copies:
        copy.wait()


def gather_back(back_refs, gathered_ref):
    slots, width = back_refs[0].shape
    for c, ref in enumerate(back_refs):
        gathered_ref[c * slots : (c + 1) * slots, :] = ref[...]
    gathered_ref[3 * slots :, :] = jnp.zeros((LANES - 3 * slots, width), BF16)


def collected(own_ref, wanted, gathered_ref, tile):
    target = jnp.broadcast_to(wanted, (LANES, LANES))
    picks = one_hot(target == iota((LANES, LANES), 0) + tile * LANES)
    own = own_ref[tile * LANES : (tile + 1) * LANES, :]
    return (own + matmul(picks, gathered_ref[...])).astype(BF16)


def middle_kernel(
    par_ref, own_ref, ba_ref, bb_ref, bc_ref, la_ref, lb_ref, lc_ref, scale_ref, jacobi_ref, z_ref,
    oa_ref, ob_ref, oc_ref, gathered_ref, v_ref
):
    wanted = wanted_row(par_ref[0], [la_ref, lb_ref, lc_ref])
    gather_back([ba_ref, bb_ref, bc_ref], gathered_ref)
    for t in range(own_ref.shape[0] // LANES):
        v_ref[t * LANES : (t + 1) * LANES, :] = collected(own_ref, wanted, gathered_ref, t)
    precondition(v_ref, scale_ref, jacobi_ref, z_ref)
    send_rows(wanted, z_ref, [oa_ref, ob_ref, oc_ref])


def last_kernel(
    par_ref, own_ref, ba_ref, bb_ref, bc_ref, la_ref, lb_ref, lc_ref, out_hbm, gathered_ref,
    out_ref, sems
):
    wanted = wanted_row(par_ref[0], [la_ref, lb_ref, lc_ref])
    gather_back([ba_ref, bb_ref, bc_ref], gathered_ref)
    copies = []
    for t in range(own_ref.shape[0] // LANES):
        span = pl.ds(t * LANES, LANES)
        out_ref[span, :] = collected(own_ref, wanted, gathered_ref, t)
        copy = pltpu.make_async_copy(out_ref.at[span, :], out_hbm.at[span, :], sems.at[t])
        copy.start()
        copies.append(copy)
    for copy in copies:
        copy.wait()


def call(kernel, operands, spaces, outs, scratch, flops, name, out_spaces=None, grant=12):
    out_spaces = out_spaces or [VMEM] * len(outs)
    moved = sum(a.size * a.dtype.itemsize for a in operands)
    return pl.pallas_call(
        kernel,
        out_shape=[jax.ShapeDtypeStruct(s, d) for s, d in outs],
        in_specs=[pl.BlockSpec(memory_space=s) for s in spaces],
        out_specs=[pl.BlockSpec(memory_space=s) for s in out_spaces],
        scratch_shapes=scratch,
        compiler_params=pltpu.CompilerParams(vmem_limit_bytes=grant * 1024 * 1024),
        cost_estimate=pl.CostEstimate(flops=flops, bytes_accessed=moved, transcendentals=0),
        name=name,
    )(*operands)


def in_hbm(array):
    return pltpu.with_memory_space_constraint(array, HBM)


def pairings(size):
    def both(pairs):
        return [pair for a, b in pairs for pair in ((a, b), (b, a))]

    even = both([(i, i + 1) for i in range(0, size - 1, 2)])
    odd = both([(i, i + 1) for i in range(1, size - 1, 2)])
    opposite = [(i, (i + size // 2) % size) for i in range(size)]
    return (opposite, odd, even)


def exchange(arrays, size, reverse=False):
    ways = pairings(size)
    order = (2, 1, 0) if reverse else (0, 1, 2)
    got = {c: lax.ppermute(arrays[c], "elem", ways[c]) for c in order}
    return [got[c] for c in range(3)]


def per_device(
    size,
    trace_rhs,
    face_scale,
    stiff_scale,
    mass_scale,
    elem_faces,
    halo_faces,
    elem_count,
    jacobi_block,
    stiffness,
    mass,
    lifting,
):
    faces, width = trace_rhs.shape
    slots = halo_faces.shape[2]
    elems = elem_faces.shape[0]
    face_dofs = jacobi_block.shape[0]
    eld, inside = lifting.shape
    pairs = width // LANES
    halo_rows = LANES
    ext_rows = faces + halo_rows
    slots_all = 6 * elems
    lists = exchange([halo_faces.transpose(1, 0, 2)] * 3, size, reverse=True)
    par = (lax.axis_index("elem") % 2).astype(I32).reshape(1)
    stiff_row = stiff_scale.reshape(1, elems)
    mass_row = mass_scale.reshape(1, elems)
    field = ((faces, width), BF16)
    rows = [((slots, width), BF16)] * 3
    x_shape = ((2 * pairs * elems, eld), BF16)
    y_shape = ((slots_all, width), BF16)
    own_shape = ((faces, width), F32)
    element_flops = 4 * 2 * pairs * elems * eld * eld

    first, weights, scale = call(
        prepare_kernel,
        [in_hbm(a) for a in (trace_rhs, jacobi_block, stiffness, mass, face_scale)],
        [HBM] * 5,
        [field, ((eld, 2 * eld), BF16), ((1, faces), F32)],
        [
            VMEM(trace_rhs.shape, BF16),
            VMEM(jacobi_block.shape, BF16),
            VMEM(face_scale.shape, F32),
            pltpu.SemaphoreType.DMA((5,)),
        ],
        2 * faces * width * 256,
        "prepare",
    )
    outgoing = call(
        send_kernel,
        [par, first, *lists],
        [SMEM] + [VMEM] * 4,
        rows,
        [],
        2 * LANES * faces * width,
        "send",
    )
    arrived = exchange(outgoing, size)
    own_pick, halo_pick, spread = call(
        functools.partial(tables_kernel, slots, faces),
        [elem_count, par, elem_faces.T],
        [SMEM, SMEM, VMEM],
        [
            ((slots_all, faces), BF16),
            ((slots_all // 2, 2 * halo_rows), BF16),
            ((ext_rows, slots_all), BF16),
        ],
        [],
        slots_all * ext_rows * 4,
        "tables",
    )

    def operator(own_x, arrived, keep_x, name):
        halo = VMEM((2 * halo_rows, 2 * width), BF16)
        return call(
            operator_kernel,
            [halo_pick, spread, own_x, *arrived, stiff_row, mass_row, weights],
            [VMEM] * 9,
            [y_shape, *rows] + ([x_shape] if keep_x else []),
            [halo] if keep_x else [VMEM(*x_shape), halo],
            element_flops,
            name,
        )

    gather_flops = 2 * slots_all * faces * width
    (own_x,) = call(
        gather_kernel, [own_pick, first], [VMEM] * 2, [x_shape], [], gather_flops, "gather1"
    )
    y, *back = operator(own_x, arrived, False, "operator1")
    returned = exchange(back, size)
    (own,) = call(
        sums_kernel,
        [spread, y],
        [VMEM] * 2,
        [own_shape],
        [],
        2 * faces * slots_all * width,
        "sums1",
    )
    second, *outgoing = call(
        middle_kernel,
        [par, own, *returned, *lists, scale, jacobi_block],
        [SMEM] + [VMEM] * 9,
        [field, *rows],
        [VMEM((LANES, width), BF16), VMEM((faces, width), BF16)],
        2 * faces * width * 256,
        "middle",
    )
    arrived = exchange(outgoing, size)
    own_x, lift = call(
        gather_lift_kernel,
        [own_pick, second, in_hbm(lifting)],
        [VMEM] * 2 + [HBM],
        [x_shape, (lifting.shape, BF16)],
        [pltpu.SemaphoreType.DMA],
        gather_flops,
        "gather2",
    )
    y, *back, x = operator(own_x, arrived, True, "operator2")
    returned = exchange(back, size)
    own, interior = call(
        finish_kernel,
        [spread, y, x, lift],
        [VMEM] * 4,
        [own_shape, ((elems, width // face_dofs * inside), BF16)],
        [
            VMEM((elems, width // face_dofs * inside), BF16),
            pltpu.SemaphoreType.DMA((pairs // 2,)),
        ],
        4 * pairs * elems * eld * inside,
        "finish",
        [VMEM, HBM],
    )
    (applied,) = call(
        last_kernel,
        [par, own, *returned, *lists],
        [SMEM] + [VMEM] * 7,
        [field],
        [
            VMEM((LANES, width), BF16),
            VMEM((faces, width), BF16),
            pltpu.SemaphoreType.DMA((faces // LANES,)),
        ],
        2 * faces * width * 128,
        "last",
        [HBM],
    )
    return (applied, interior)


def solution(mesh):
    rows = P(("grp", "elem", "sub"))
    split = P(("grp", "elem", "sub"), "src")
    in_specs = (
        split,
        rows,
        rows,
        rows,
        P(("grp", "elem", "sub"), None),
        P(("grp", "elem", "sub"), None, None),
        rows,
        P(),
        P(),
        P(),
        P(),
    )
    return jax.shard_map(
        functools.partial(per_device, mesh.shape["elem"]),
        mesh=mesh,
        in_specs=in_specs,
        out_specs=(split, split),
        check_vma=False,
    )
```

```python
import functools

import jax
import jax.numpy as jnp
from jax import lax
from jax.experimental import pallas as pl
from jax.experimental.pallas import tpu as pltpu
from jax.sharding import PartitionSpec as P

F32 = jnp.float32
BF16 = jnp.bfloat16
I32 = jnp.int32
LANES = 128
VMEM = pltpu.VMEM
SMEM = pltpu.SMEM
HBM = pltpu.HBM


def iota(shape, dim):
    return lax.broadcasted_iota(I32, shape, dim)


def one_hot(condition):
    return jnp.where(condition, 1.0, 0.0).astype(BF16)


def matmul(a, b):
    return jnp.dot(a, b, preferred_element_type=F32)


def column_tiles(row):
    count = row.shape[1] // LANES
    return [
        jnp.transpose(
            jnp.broadcast_to(row[:, t * LANES : (t + 1) * LANES].astype(F32), (LANES, LANES))
        )
        for t in range(count)
    ]


def block_diagonal(block, copies):
    rows, cols = block.shape
    wide = jnp.concatenate([block] * copies, axis=1)
    full = jnp.concatenate([wide] * copies, axis=0)
    shape = (rows * copies, cols * copies)
    keep = (iota(shape, 0) // rows) == (iota(shape, 1) // cols)
    return jnp.where(keep, full, jnp.zeros_like(full))


def precondition(field_ref, scale_ref, block_ref, z_ref):
    step = block_ref.shape[0]
    scale = scale_ref[...]
    scale = jnp.concatenate([scale] * (step // LANES), axis=1)
    for start in range(0, field_ref.shape[1], step):
        product = matmul(field_ref[:, start : start + step], block_ref[...])
        z_ref[:, start : start + step] = (product * scale).astype(BF16)


def swap_halves(even, odd, low):
    turn = lambda tile: pltpu.roll(tile, LANES // 2, 1)
    return jnp.where(low, even, turn(odd)), jnp.where(low, turn(even), odd)


def prepare_kernel(
    rhs_hbm, jacobi_hbm, scale_hbm, stiff_hbm, mass_hbm,
    z_ref, block_ref, scale_ref, face_scale_ref, w_ref, rhs_ref, small_ref, line_ref, sems
):
    half = w_ref.shape[1] // 2
    sources = (jacobi_hbm, scale_hbm, rhs_hbm, stiff_hbm, mass_hbm)
    targets = (small_ref, line_ref, rhs_ref, w_ref.at[:, :half], w_ref.at[:, half:])
    copies = [
        pltpu.make_async_copy(src, dst, sems.at[i])
        for i, (src, dst) in enumerate(zip(sources, targets))
    ]
    for copy in copies:
        copy.start()
    copies[0].wait()
    block_ref[...] = block_diagonal(small_ref[...].astype(F32), 4).astype(BF16)
    copies[1].wait()
    scale_ref[...] = line_ref[...].reshape(scale_ref.shape)
    for t, tile in enumerate(column_tiles(scale_ref[...])):
        face_scale_ref[t * LANES : (t + 1) * LANES, :] = tile
    copies[2].wait()
    precondition(rhs_ref, face_scale_ref, block_ref, z_ref)
    copies[3].wait()
    copies[4].wait()


def wanted_part(par, list_ref, colour):
    if colour == 0:
        return list_ref[2]
    return jnp.where(par == 2 - colour, list_ref[0], list_ref[1])


def padded(row):
    return jnp.concatenate([row, jnp.full((1, LANES - row.shape[1]), -1, I32)], axis=1)


def wanted_row(par, list_refs):
    parts = [wanted_part(par, ref, c) for c, ref in enumerate(list_refs)]
    return padded(jnp.concatenate(parts, axis=1))


def wanted_tables(wanted, scale_row):
    (column,) = column_tiles(wanted)
    column = column.astype(I32)
    lane = iota((LANES, LANES), 1)
    picks = []
    scale = jnp.zeros((LANES, LANES), F32)
    for t in range(scale_row.shape[1] // LANES):
        chosen = column == lane + t * LANES
        picks.append(one_hot(chosen))
        across = jnp.broadcast_to(scale_row[:, t * LANES : (t + 1) * LANES], (LANES, LANES))
        scale = scale + jnp.where(chosen, across, 0.0)
    scale = jnp.broadcast_to(jnp.sum(scale, axis=1, keepdims=True), (LANES, LANES))
    return jnp.concatenate(picks, axis=1), scale


def send_rows(rows, scale, block_ref, out_refs):
    step = block_ref.shape[0]
    scale = jnp.concatenate([scale] * (step // LANES), axis=1)
    slots = out_refs[0].shape[0]
    for start in range(0, rows.shape[1], step):
        product = matmul(rows[:, start : start + step], block_ref[...])
        product = (product * scale).astype(BF16)
        for c, ref in enumerate(out_refs):
            ref[:, start : start + step] = product[c * slots : (c + 1) * slots, :]


def send_kernel(par_ref, z_ref, ec_ref, eb_ref, ea_ref, *out_refs):
    (column,) = column_tiles(wanted_row(par_ref[0], [ea_ref, eb_ref, ec_ref]))
    column = column.astype(I32)
    lane = iota((LANES, LANES), 1)
    tiles = range(z_ref.shape[0] // LANES)
    pick = jnp.concatenate([one_hot(column == lane + t * LANES) for t in tiles], axis=1)
    rows = matmul(pick, z_ref[...]).astype(BF16)
    slots = out_refs[0].shape[0]
    for c, ref in enumerate(out_refs):
        ref[...] = rows[c * slots : (c + 1) * slots, :]


def column_ids(par, faces, slots, tile, axis):
    index = iota((LANES, LANES), axis) + tile * LANES
    moved = jnp.where(index < faces + slots, 2 * slots, slots * par - slots)
    moved = jnp.where(index < faces + 2 * slots, moved, -slots - slots * par)
    return jnp.where(index < faces, index, index + moved)


def element_tables(par, slots, count, ids_ref, own_ref, halo_ref, spread_ref):
    ids_all = jnp.where(iota(ids_ref.shape, 1) < count, ids_ref[...], -1)
    tiles = spread_ref.shape[0] // LANES
    faces = own_ref.shape[1]
    owned = faces // LANES
    lanes = [column_ids(par, faces, slots, t, 1) for t in range(tiles)]
    rows = [column_ids(par, faces, slots, t, 0) for t in range(tiles)]
    span = lambda i: slice(i * LANES, (i + 1) * LANES)
    for k in range(ids_ref.shape[0]):
        across = jnp.broadcast_to(ids_all[k : k + 1, :], (LANES, LANES))
        down = jnp.transpose(across.astype(F32)).astype(I32)
        for t in range(tiles):
            pick = one_hot(down == lanes[t])
            if t < owned:
                own_ref[span(k), span(t)] = pick
            else:
                halo_ref[span(k // 2), span(k % 2)] = pick
            spread_ref[span(t), span(k)] = one_hot(across == rows[t])


def gather_own(pick_ref, z_ref, x_ref):
    width = z_ref.shape[1]
    low = iota((LANES, LANES), 1) < LANES // 2
    for t in range(x_ref.shape[1] // LANES):
        rows = matmul(pick_ref[2 * t * LANES : 2 * (t + 1) * LANES, :], z_ref[...])
        for p in range(width // LANES):
            pair = rows[:, p * LANES : (p + 1) * LANES]
            even, odd = swap_halves(pair[:LANES], pair[LANES:], low)
            at = 2 * p * LANES
            x_ref[at : at + LANES, t * LANES : (t + 1) * LANES] = even.astype(BF16)
            x_ref[at + LANES : at + 2 * LANES, t * LANES : (t + 1) * LANES] = odd.astype(BF16)


def first_gather_kernel(
    slots, par_ref, count_ref, z_ref, ids_ref, stiff_scale_ref, mass_scale_ref,
    x_ref, own_ref, halo_ref, spread_ref, element_scale_ref
):
    element_tables(par_ref[0], slots, count_ref[0], ids_ref, own_ref, halo_ref, spread_ref)
    gather_own(own_ref, z_ref, x_ref)
    (element_scale_ref[0],) = column_tiles(stiff_scale_ref[...])
    (element_scale_ref[1],) = column_tiles(mass_scale_ref[...])


def second_gather_kernel(
    pick_ref, sums_ref, ba_ref, bb_ref, bc_ref, give_ref, scale_ref, block_ref, lift_hbm,
    x_ref, lift_ref, gathered_ref, v_ref, z_ref, sem
):
    load = pltpu.make_async_copy(lift_hbm, lift_ref, sem)
    load.start()
    gather_back([ba_ref, bb_ref, bc_ref], gathered_ref)
    for t in range(sums_ref.shape[0] // LANES):
        v_ref[t * LANES : (t + 1) * LANES, :] = collected(sums_ref, give_ref, gathered_ref, t)
    precondition(v_ref, scale_ref, block_ref, z_ref)
    gather_own(pick_ref, z_ref, x_ref)
    load.wait()


def operator_kernel(
    pick_ref, spread_ref, own_x_ref, aa_ref, ab_ref, ac_ref, scale_ref,
    w_ref, y_ref, ba_ref, bb_ref, bc_ref, x_ref, halo_ref
):
    slots, width = aa_ref.shape
    pairs = width // LANES
    filled = 3 * slots
    arrived = jnp.concatenate([aa_ref[...], ab_ref[...], ac_ref[...]], axis=0).astype(F32)
    low = iota((filled, LANES), 1) < LANES // 2
    zero = jnp.zeros((filled, LANES), F32)
    for first in (0, LANES):
        halo_ref[first + filled : first + LANES, :] = jnp.zeros(
            (LANES - filled, halo_ref.shape[1]), BF16
        )
    for p in range(pairs):
        tile = arrived[:, p * LANES : (p + 1) * LANES]
        turned = pltpu.roll(tile, LANES // 2, 1)
        even = slice(2 * p * LANES, (2 * p + 1) * LANES)
        odd = slice((2 * p + 1) * LANES, (2 * p + 2) * LANES)
        halo_ref[:filled, even] = jnp.where(low, tile, zero).astype(BF16)
        halo_ref[LANES : LANES + filled, even] = jnp.where(low, zero, turned).astype(BF16)
        halo_ref[:filled, odd] = jnp.where(low, turned, zero).astype(BF16)
        halo_ref[LANES : LANES + filled, odd] = jnp.where(low, zero, tile).astype(BF16)
    for t in range(x_ref.shape[1] // LANES):
        rows = matmul(pick_ref[t * LANES : (t + 1) * LANES, :], halo_ref[...]).astype(BF16)
        for s in range(2 * pairs):
            at = (slice(s * LANES, (s + 1) * LANES), slice(t * LANES, (t + 1) * LANES))
            x_ref[at] = own_x_ref[at] + rows[:, s * LANES : (s + 1) * LANES]
    stiff = jnp.concatenate([scale_ref[0]] * 2, axis=0)
    mass = jnp.concatenate([scale_ref[1]] * 2, axis=0)
    low = iota((LANES, LANES), 1) < LANES // 2
    half = w_ref.shape[1] // 2
    for p in range(pairs):
        product = matmul(x_ref[2 * p * LANES : 2 * (p + 1) * LANES, :], w_ref[...])
        for t in range(half // LANES):
            at = t * LANES
            term = (
                stiff * product[:, at : at + LANES]
                - mass * product[:, half + at : half + at + LANES]
            )
            first, second = swap_halves(term[:LANES], term[LANES:], low)
            place = slice(p * LANES, (p + 1) * LANES)
            y_ref[2 * at : 2 * at + LANES, place] = first.astype(BF16)
            y_ref[2 * at + LANES : 2 * at + 2 * LANES, place] = second.astype(BF16)
    rows = matmul(spread_ref[spread_ref.shape[0] - LANES :, :], y_ref[...]).astype(BF16)
    for c, ref in enumerate((ba_ref, bb_ref, bc_ref)):
        ref[...] = rows[c * slots : (c + 1) * slots, :]


def own_sums(spread_ref, y_ref, own_ref):
    for t in range(own_ref.shape[0] // LANES):
        own_ref[t * LANES : (t + 1) * LANES, :] = matmul(
            spread_ref[t * LANES : (t + 1) * LANES, :], y_ref[...]
        )


def sums_kernel(
    par_ref, spread_ref, y_ref, ec_ref, eb_ref, ea_ref, scale_ref,
    own_ref, rows_ref, same_ref, give_ref, request_scale_ref, high_ref, low_ref
):
    wanted = wanted_row(par_ref[0], [ea_ref, eb_ref, ec_ref])
    request, request_scale_ref[...] = wanted_tables(wanted, scale_ref[...])
    target = jnp.broadcast_to(wanted, give_ref.shape)
    give_ref[...] = one_hot(target == iota(give_ref.shape, 0))
    own_sums(spread_ref, y_ref, own_ref)
    same_ref[...] = matmul(request, give_ref[...]).astype(BF16)
    high_ref[...] = own_ref[...].astype(BF16)
    low_ref[...] = (own_ref[...] - high_ref[...].astype(F32)).astype(BF16)
    rows_ref[...] = matmul(request, high_ref[...])
    rows_ref[...] += matmul(request, low_ref[...])


def finish_kernel(
    spread_ref, y_ref, x_ref, lift_ref, own_ref, interior_hbm, inside_ref, sems
):
    wide = lift_ref.shape[1]
    step = 4
    copies = []
    for start in range(0, x_ref.shape[0] // LANES, step):
        rows = x_ref[start * LANES : (start + step) * LANES, :]
        product = matmul(rows, lift_ref[...]).astype(BF16)
        for r in range(step):
            inside_ref[:, (start + r) * wide : (start + r + 1) * wide] = product[
                r * LANES : (r + 1) * LANES, :
            ]
        span = pl.ds(start * wide, step * wide)
        copy = pltpu.make_async_copy(
            inside_ref.at[:, span], interior_hbm.at[:, span], sems.at[len(copies)]
        )
        copy.start()
        copies.append(copy)
    own_sums(spread_ref, y_ref, own_ref)
    for copy in copies:
        copy.wait()


def gather_back(back_refs, gathered_ref):
    slots, width = back_refs[0].shape
    for c, ref in enumerate(back_refs):
        gathered_ref[c * slots : (c + 1) * slots, :] = ref[...]
    gathered_ref[3 * slots :, :] = jnp.zeros((LANES - 3 * slots, width), BF16)


def collected(own_ref, give_ref, gathered_ref, tile):
    rows = slice(tile * LANES, (tile + 1) * LANES)
    return (own_ref[rows, :] + matmul(give_ref[rows, :], gathered_ref[...])).astype(BF16)


def middle_kernel(
    rows_ref, ba_ref, bb_ref, bc_ref, same_ref, request_scale_ref, block_ref,
    oa_ref, ob_ref, oc_ref, gathered_ref
):
    gather_back([ba_ref, bb_ref, bc_ref], gathered_ref)
    rows = (rows_ref[...] + matmul(same_ref[...], gathered_ref[...])).astype(BF16)
    send_rows(rows, request_scale_ref[...], block_ref, [oa_ref, ob_ref, oc_ref])


def last_kernel(
    own_ref, ba_ref, bb_ref, bc_ref, give_ref, out_hbm, gathered_ref, out_ref, sems
):
    gather_back([ba_ref, bb_ref, bc_ref], gathered_ref)
    copies = []
    for t in range(own_ref.shape[0] // LANES):
        span = pl.ds(t * LANES, LANES)
        out_ref[span, :] = collected(own_ref, give_ref, gathered_ref, t)
        copy = pltpu.make_async_copy(out_ref.at[span, :], out_hbm.at[span, :], sems.at[t])
        copy.start()
        copies.append(copy)
    for copy in copies:
        copy.wait()


def call(kernel, operands, spaces, outs, scratch, flops, name, out_spaces=None, grant=12):
    out_spaces = out_spaces or [VMEM] * len(outs)
    moved = sum(a.size * a.dtype.itemsize for a in operands)
    return pl.pallas_call(
        kernel,
        out_shape=[jax.ShapeDtypeStruct(s, d) for s, d in outs],
        in_specs=[pl.BlockSpec(memory_space=s) for s in spaces],
        out_specs=[pl.BlockSpec(memory_space=s) for s in out_spaces],
        scratch_shapes=scratch,
        compiler_params=pltpu.CompilerParams(vmem_limit_bytes=grant * 1024 * 1024),
        cost_estimate=pl.CostEstimate(flops=flops, bytes_accessed=moved, transcendentals=0),
        name=name,
    )(*operands)


def in_hbm(array):
    return pltpu.with_memory_space_constraint(array, HBM)


def pairings(size):
    def both(pairs):
        return [pair for a, b in pairs for pair in ((a, b), (b, a))]

    even = both([(i, i + 1) for i in range(0, size - 1, 2)])
    odd = both([(i, i + 1) for i in range(1, size - 1, 2)])
    opposite = [(i, (i + size // 2) % size) for i in range(size)]
    return (opposite, odd, even)


def exchange(arrays, size, reverse=False):
    ways = pairings(size)
    order = (2, 1, 0) if reverse else (0, 1, 2)
    got = {c: lax.ppermute(arrays[c], "elem", ways[c]) for c in order}
    return [got[c] for c in range(3)]


def per_device(
    size,
    trace_rhs,
    face_scale,
    stiff_scale,
    mass_scale,
    elem_faces,
    halo_faces,
    elem_count,
    jacobi_block,
    stiffness,
    mass,
    lifting,
):
    faces, width = trace_rhs.shape
    slots = halo_faces.shape[2]
    elems = elem_faces.shape[0]
    face_dofs = jacobi_block.shape[0]
    eld, inside = lifting.shape
    pairs = width // LANES
    halo_rows = LANES
    ext_rows = faces + halo_rows
    slots_all = 6 * elems
    lists = exchange([halo_faces.transpose(1, 0, 2)] * 3, size, reverse=True)
    par = (lax.axis_index("elem") % 2).astype(I32).reshape(1)
    stiff_row = stiff_scale.reshape(1, elems)
    mass_row = mass_scale.reshape(1, elems)
    field = ((faces, width), BF16)
    rows = [((slots, width), BF16)] * 3
    x_shape = ((2 * pairs * elems, eld), BF16)
    y_shape = ((slots_all, width), BF16)
    own_shape = ((faces, width), F32)
    element_flops = 4 * 2 * pairs * elems * eld * eld

    step = 4 * face_dofs
    first, block, scale, face_scales, weights = call(
        prepare_kernel,
        [in_hbm(a) for a in (trace_rhs, jacobi_block, face_scale, stiffness, mass)],
        [HBM] * 5,
        [
            field,
            ((step, step), BF16),
            ((1, faces), F32),
            ((faces, LANES), F32),
            ((eld, 2 * eld), BF16),
        ],
        [
            VMEM(*field),
            VMEM(jacobi_block.shape, BF16),
            VMEM(face_scale.shape, F32),
            pltpu.SemaphoreType.DMA((5,)),
        ],
        2 * faces * width * 256,
        "prepare",
    )
    outgoing = call(
        send_kernel,
        [par, first, *lists[::-1]],
        [SMEM] + [VMEM] * 4,
        rows,
        [],
        2 * LANES * faces * width,
        "send",
    )
    arrived = exchange(outgoing, size)
    gather_flops = 2 * slots_all * faces * width
    tile = (LANES, LANES)
    own_x, own_pick, halo_pick, spread, element_scales = call(
        functools.partial(first_gather_kernel, slots),
        [par, elem_count, first, elem_faces.T, stiff_row, mass_row],
        [SMEM] * 2 + [VMEM] * 4,
        [
            x_shape,
            ((slots_all, faces), BF16),
            ((slots_all // 2, 2 * halo_rows), BF16),
            ((ext_rows, slots_all), BF16),
            ((2, *tile), F32),
        ],
        [],
        gather_flops,
        "gather1",
    )

    def operator(own_x, arrived, keep_x, name):
        halo = VMEM((2 * halo_rows, 2 * width), BF16)
        return call(
            operator_kernel,
            [halo_pick, spread, own_x, *arrived, element_scales, weights],
            [VMEM] * 8,
            [y_shape, *rows] + ([x_shape] if keep_x else []),
            [halo] if keep_x else [VMEM(*x_shape), halo],
            element_flops,
            name,
        )

    y, *back = operator(own_x, arrived, False, "operator1")
    returned = exchange(back, size)
    own, own_rows, same, give, request_scale = call(
        sums_kernel,
        [par, spread, y, *lists[::-1], scale],
        [SMEM] + [VMEM] * 6,
        [
            own_shape,
            ((LANES, width), F32),
            (tile, BF16),
            ((faces, LANES), BF16),
            (tile, F32),
        ],
        [VMEM(*field)] * 2,
        2 * faces * slots_all * width,
        "sums1",
    )
    outgoing = call(
        middle_kernel,
        [own_rows, *returned, same, request_scale, block],
        [VMEM] * 7,
        rows,
        [VMEM((LANES, width), BF16)],
        2 * LANES * width * 256,
        "middle",
    )
    arrived = exchange(outgoing, size)
    own_x, lift = call(
        second_gather_kernel,
        [own_pick, own, *returned, give, face_scales, block, in_hbm(lifting)],
        [VMEM] * 8 + [HBM],
        [x_shape, (lifting.shape, BF16)],
        [VMEM((LANES, width), BF16), VMEM(*field), VMEM(*field), pltpu.SemaphoreType.DMA],
        gather_flops,
        "gather2",
    )
    y, *back, x = operator(own_x, arrived, True, "operator2")
    returned = exchange(back, size)
    own, interior = call(
        finish_kernel,
        [spread, y, x, lift],
        [VMEM] * 4,
        [own_shape, ((elems, width // face_dofs * inside), BF16)],
        [
            VMEM((elems, width // face_dofs * inside), BF16),
            pltpu.SemaphoreType.DMA((pairs // 2,)),
        ],
        4 * pairs * elems * eld * inside,
        "finish",
        [VMEM, HBM],
    )
    (applied,) = call(
        last_kernel,
        [own, *returned, give],
        [VMEM] * 5,
        [field],
        [
            VMEM((LANES, width), BF16),
            VMEM((faces, width), BF16),
            pltpu.SemaphoreType.DMA((faces // LANES,)),
        ],
        2 * faces * width * 128,
        "last",
        [HBM],
    )
    return (applied, interior)


def solution(mesh):
    rows = P(("grp", "elem", "sub"))
    split = P(("grp", "elem", "sub"), "src")
    in_specs = (
        split,
        rows,
        rows,
        rows,
        P(("grp", "elem", "sub"), None),
        P(("grp", "elem", "sub"), None, None),
        rows,
        P(),
        P(),
        P(),
        P(),
    )
    return jax.shard_map(
        functools.partial(per_device, mesh.shape["elem"]),
        mesh=mesh,
        in_specs=in_specs,
        out_specs=(split, split),
        check_vma=False,
    )
```

```python
import functools

import jax
import jax.numpy as jnp
from jax import lax
from jax.experimental import pallas as pl
from jax.experimental.pallas import tpu as pltpu
from jax.sharding import PartitionSpec as P

F32 = jnp.float32
BF16 = jnp.bfloat16
I32 = jnp.int32
LANES = 128
VMEM = pltpu.VMEM
SMEM = pltpu.SMEM
HBM = pltpu.HBM


def iota(shape, dim):
    return lax.broadcasted_iota(I32, shape, dim)


def one_hot(condition):
    return jnp.where(condition, 1.0, 0.0).astype(BF16)


def matmul(a, b):
    return jnp.dot(a, b, preferred_element_type=F32)


def column_tiles(row):
    count = row.shape[1] // LANES
    return [
        jnp.transpose(
            jnp.broadcast_to(row[:, t * LANES : (t + 1) * LANES].astype(F32), (LANES, LANES))
        )
        for t in range(count)
    ]


def block_diagonal(block, copies):
    rows, cols = block.shape
    wide = jnp.concatenate([block] * copies, axis=1)
    full = jnp.concatenate([wide] * copies, axis=0)
    shape = (rows * copies, cols * copies)
    keep = (iota(shape, 0) // rows) == (iota(shape, 1) // cols)
    return jnp.where(keep, full, jnp.zeros_like(full))


def precondition(field_ref, scale_ref, block_ref, z_ref):
    step = block_ref.shape[0]
    scale = scale_ref[...]
    scale = jnp.concatenate([scale] * (step // LANES), axis=1)
    for start in range(0, field_ref.shape[1], step):
        product = matmul(field_ref[:, start : start + step], block_ref[...])
        z_ref[:, start : start + step] = (product * scale).astype(BF16)


def swap_halves(even, odd, low):
    turn = lambda tile: pltpu.roll(tile, LANES // 2, 1)
    return jnp.where(low, even, turn(odd)), jnp.where(low, turn(even), odd)


def prepare_kernel(
    rhs_hbm, jacobi_hbm, scale_hbm, stiff_hbm, mass_hbm,
    z_ref, block_ref, scale_ref, face_scale_ref, w_ref, rhs_ref, small_ref, line_ref, sems
):
    half = w_ref.shape[1] // 2
    sources = (jacobi_hbm, scale_hbm, rhs_hbm, stiff_hbm, mass_hbm)
    targets = (small_ref, line_ref, rhs_ref, w_ref.at[:, :half], w_ref.at[:, half:])
    copies = [
        pltpu.make_async_copy(src, dst, sems.at[i])
        for i, (src, dst) in enumerate(zip(sources, targets))
    ]
    for copy in copies:
        copy.start()
    copies[0].wait()
    block_ref[...] = block_diagonal(small_ref[...].astype(F32), 4).astype(BF16)
    copies[1].wait()
    scale_ref[...] = line_ref[...].reshape(scale_ref.shape)
    for t, tile in enumerate(column_tiles(scale_ref[...])):
        face_scale_ref[t * LANES : (t + 1) * LANES, :] = tile
    copies[2].wait()
    precondition(rhs_ref, face_scale_ref, block_ref, z_ref)
    copies[3].wait()
    copies[4].wait()


def wanted_part(par, list_ref, colour):
    if colour == 0:
        return list_ref[2]
    return jnp.where(par == 2 - colour, list_ref[0], list_ref[1])


def padded(row):
    return jnp.concatenate([row, jnp.full((1, LANES - row.shape[1]), -1, I32)], axis=1)


def wanted_row(par, list_refs):
    parts = [wanted_part(par, ref, c) for c, ref in enumerate(list_refs)]
    return padded(jnp.concatenate(parts, axis=1))


def wanted_tables(wanted, scale_row):
    (column,) = column_tiles(wanted)
    column = column.astype(I32)
    lane = iota((LANES, LANES), 1)
    picks = []
    scale = jnp.zeros((LANES, LANES), F32)
    for t in range(scale_row.shape[1] // LANES):
        chosen = column == lane + t * LANES
        picks.append(one_hot(chosen))
        across = jnp.broadcast_to(scale_row[:, t * LANES : (t + 1) * LANES], (LANES, LANES))
        scale = scale + jnp.where(chosen, across, 0.0)
    scale = jnp.broadcast_to(jnp.sum(scale, axis=1, keepdims=True), (LANES, LANES))
    return jnp.concatenate(picks, axis=1), scale


def send_rows(rows, scale, block_ref, out_refs):
    step = block_ref.shape[0]
    scale = jnp.concatenate([scale] * (step // LANES), axis=1)
    slots = out_refs[0].shape[0]
    for start in range(0, rows.shape[1], step):
        product = matmul(rows[:, start : start + step], block_ref[...])
        product = (product * scale).astype(BF16)
        for c, ref in enumerate(out_refs):
            ref[:, start : start + step] = product[c * slots : (c + 1) * slots, :]


def send_kernel(par_ref, z_ref, ec_ref, eb_ref, ea_ref, *out_refs):
    (column,) = column_tiles(wanted_row(par_ref[0], [ea_ref, eb_ref, ec_ref]))
    column = column.astype(I32)
    lane = iota((LANES, LANES), 1)
    tiles = range(z_ref.shape[0] // LANES)
    pick = jnp.concatenate([one_hot(column == lane + t * LANES) for t in tiles], axis=1)
    rows = matmul(pick, z_ref[...]).astype(BF16)
    slots = out_refs[0].shape[0]
    for c, ref in enumerate(out_refs):
        ref[...] = rows[c * slots : (c + 1) * slots, :]


def column_ids(par, faces, slots, tile, axis):
    index = iota((LANES, LANES), axis) + tile * LANES
    moved = jnp.where(index < faces + slots, 2 * slots, slots * par - slots)
    moved = jnp.where(index < faces + 2 * slots, moved, -slots - slots * par)
    return jnp.where(index < faces, index, index + moved)


def element_tables(par, slots, count, ids_ref, own_ref, halo_ref, spread_ref):
    ids_all = jnp.where(iota(ids_ref.shape, 1) < count, ids_ref[...], -1)
    tiles = spread_ref.shape[0] // LANES
    faces = own_ref.shape[1]
    owned = faces // LANES
    lanes = [column_ids(par, faces, slots, t, 1) for t in range(tiles)]
    rows = [column_ids(par, faces, slots, t, 0) for t in range(tiles)]
    span = lambda i: slice(i * LANES, (i + 1) * LANES)
    for k in range(ids_ref.shape[0]):
        across = jnp.broadcast_to(ids_all[k : k + 1, :], (LANES, LANES))
        down = jnp.transpose(across.astype(F32)).astype(I32)
        for t in range(tiles):
            pick = one_hot(down == lanes[t])
            if t < owned:
                own_ref[span(k), span(t)] = pick
            else:
                halo_ref[span(k // 2), span(k % 2)] = pick
            spread_ref[span(t), span(k)] = one_hot(across == rows[t])


def gather_own(pick_ref, z_ref, x_ref):
    width = z_ref.shape[1]
    low = iota((LANES, LANES), 1) < LANES // 2
    for t in range(x_ref.shape[1] // LANES):
        rows = matmul(pick_ref[2 * t * LANES : 2 * (t + 1) * LANES, :], z_ref[...])
        for p in range(width // LANES):
            pair = rows[:, p * LANES : (p + 1) * LANES]
            even, odd = swap_halves(pair[:LANES], pair[LANES:], low)
            at = 2 * p * LANES
            x_ref[at : at + LANES, t * LANES : (t + 1) * LANES] = even.astype(BF16)
            x_ref[at + LANES : at + 2 * LANES, t * LANES : (t + 1) * LANES] = odd.astype(BF16)


def first_gather_kernel(
    slots, par_ref, count_ref, z_ref, ids_ref, stiff_scale_ref, mass_scale_ref,
    x_ref, own_ref, halo_ref, spread_ref, element_scale_ref
):
    element_tables(par_ref[0], slots, count_ref[0], ids_ref, own_ref, halo_ref, spread_ref)
    gather_own(own_ref, z_ref, x_ref)
    (element_scale_ref[0],) = column_tiles(stiff_scale_ref[...])
    (element_scale_ref[1],) = column_tiles(mass_scale_ref[...])


def second_gather_kernel(
    pick_ref, sums_ref, ba_ref, bb_ref, bc_ref, give_ref, scale_ref, block_ref, lift_hbm,
    x_ref, lift_ref, gathered_ref, v_ref, z_ref, sem
):
    load = pltpu.make_async_copy(lift_hbm, lift_ref, sem)
    load.start()
    gather_back([ba_ref, bb_ref, bc_ref], gathered_ref)
    for t in range(sums_ref.shape[0] // LANES):
        v_ref[t * LANES : (t + 1) * LANES, :] = collected(sums_ref, give_ref, gathered_ref, t)
    precondition(v_ref, scale_ref, block_ref, z_ref)
    gather_own(pick_ref, z_ref, x_ref)
    load.wait()


def operator_kernel(
    pick_ref, spread_ref, own_x_ref, aa_ref, ab_ref, ac_ref, scale_ref,
    w_ref, y_ref, ba_ref, bb_ref, bc_ref, x_ref, halo_ref
):
    slots, width = aa_ref.shape
    pairs = width // LANES
    filled = 3 * slots
    arrived = jnp.concatenate([aa_ref[...], ab_ref[...], ac_ref[...]], axis=0).astype(F32)
    low = iota((filled, LANES), 1) < LANES // 2
    zero = jnp.zeros((filled, LANES), F32)
    for first in (0, LANES):
        halo_ref[first + filled : first + LANES, :] = jnp.zeros(
            (LANES - filled, halo_ref.shape[1]), BF16
        )
    for p in range(pairs):
        tile = arrived[:, p * LANES : (p + 1) * LANES]
        turned = pltpu.roll(tile, LANES // 2, 1)
        even = slice(2 * p * LANES, (2 * p + 1) * LANES)
        odd = slice((2 * p + 1) * LANES, (2 * p + 2) * LANES)
        halo_ref[:filled, even] = jnp.where(low, tile, zero).astype(BF16)
        halo_ref[LANES : LANES + filled, even] = jnp.where(low, zero, turned).astype(BF16)
        halo_ref[:filled, odd] = jnp.where(low, turned, zero).astype(BF16)
        halo_ref[LANES : LANES + filled, odd] = jnp.where(low, zero, tile).astype(BF16)
    for t in range(x_ref.shape[1] // LANES):
        rows = matmul(pick_ref[t * LANES : (t + 1) * LANES, :], halo_ref[...]).astype(BF16)
        for s in range(2 * pairs):
            at = (slice(s * LANES, (s + 1) * LANES), slice(t * LANES, (t + 1) * LANES))
            x_ref[at] = own_x_ref[at] + rows[:, s * LANES : (s + 1) * LANES]
    stiff = jnp.concatenate([scale_ref[0]] * 2, axis=0)
    mass = jnp.concatenate([scale_ref[1]] * 2, axis=0)
    low = iota((LANES, LANES), 1) < LANES // 2
    half = w_ref.shape[1] // 2
    for p in range(pairs):
        product = matmul(x_ref[2 * p * LANES : 2 * (p + 1) * LANES, :], w_ref[...])
        for t in range(half // LANES):
            at = t * LANES
            term = (
                stiff * product[:, at : at + LANES]
                - mass * product[:, half + at : half + at + LANES]
            )
            first, second = swap_halves(term[:LANES], term[LANES:], low)
            place = slice(p * LANES, (p + 1) * LANES)
            y_ref[2 * at : 2 * at + LANES, place] = first.astype(BF16)
            y_ref[2 * at + LANES : 2 * at + 2 * LANES, place] = second.astype(BF16)
    rows = matmul(spread_ref[spread_ref.shape[0] - LANES :, :], y_ref[...]).astype(BF16)
    for c, ref in enumerate((ba_ref, bb_ref, bc_ref)):
        ref[...] = rows[c * slots : (c + 1) * slots, :]


def own_sums(spread_ref, y_ref, own_ref):
    for t in range(own_ref.shape[0] // LANES):
        own_ref[t * LANES : (t + 1) * LANES, :] = matmul(
            spread_ref[t * LANES : (t + 1) * LANES, :], y_ref[...]
        )


def sums_kernel(
    par_ref, spread_ref, y_ref, ec_ref, eb_ref, ea_ref, scale_ref,
    own_ref, rows_ref, same_ref, give_ref, request_scale_ref, high_ref, low_ref
):
    wanted = wanted_row(par_ref[0], [ea_ref, eb_ref, ec_ref])
    request, request_scale_ref[...] = wanted_tables(wanted, scale_ref[...])
    target = jnp.broadcast_to(wanted, give_ref.shape)
    give_ref[...] = one_hot(target == iota(give_ref.shape, 0))
    own_sums(spread_ref, y_ref, own_ref)
    same_ref[...] = matmul(request, give_ref[...]).astype(BF16)
    high_ref[...] = own_ref[...].astype(BF16)
    low_ref[...] = (own_ref[...] - high_ref[...].astype(F32)).astype(BF16)
    rows_ref[...] = matmul(request, high_ref[...])
    rows_ref[...] += matmul(request, low_ref[...])


def finish_kernel(
    spread_ref, y_ref, x_ref, lift_ref, own_ref, interior_hbm, inside_ref, sems
):
    wide = lift_ref.shape[1]
    step = 4
    copies = []
    for start in range(0, x_ref.shape[0] // LANES, step):
        rows = x_ref[start * LANES : (start + step) * LANES, :]
        product = matmul(rows, lift_ref[...]).astype(BF16)
        for r in range(step):
            inside_ref[:, (start + r) * wide : (start + r + 1) * wide] = product[
                r * LANES : (r + 1) * LANES, :
            ]
        span = pl.ds(start * wide, step * wide)
        copy = pltpu.make_async_copy(
            inside_ref.at[:, span], interior_hbm.at[:, span], sems.at[len(copies)]
        )
        copy.start()
        copies.append(copy)
    own_sums(spread_ref, y_ref, own_ref)
    for copy in copies:
        copy.wait()


def gather_back(back_refs, gathered_ref):
    slots, width = back_refs[0].shape
    for c, ref in enumerate(back_refs):
        gathered_ref[c * slots : (c + 1) * slots, :] = ref[...]
    gathered_ref[3 * slots :, :] = jnp.zeros((LANES - 3 * slots, width), BF16)


def collected(own_ref, give_ref, gathered_ref, tile):
    rows = slice(tile * LANES, (tile + 1) * LANES)
    return (own_ref[rows, :] + matmul(give_ref[rows, :], gathered_ref[...])).astype(BF16)


def middle_kernel(
    rows_ref, ba_ref, bb_ref, bc_ref, same_ref, request_scale_ref, block_ref,
    oa_ref, ob_ref, oc_ref, gathered_ref
):
    gather_back([ba_ref, bb_ref, bc_ref], gathered_ref)
    rows = (rows_ref[...] + matmul(same_ref[...], gathered_ref[...])).astype(BF16)
    send_rows(rows, request_scale_ref[...], block_ref, [oa_ref, ob_ref, oc_ref])


def last_kernel(
    own_ref, ba_ref, bb_ref, bc_ref, give_ref, out_hbm, gathered_ref, out_ref, sems
):
    gather_back([ba_ref, bb_ref, bc_ref], gathered_ref)
    copies = []
    for t in range(own_ref.shape[0] // LANES):
        span = pl.ds(t * LANES, LANES)
        out_ref[span, :] = collected(own_ref, give_ref, gathered_ref, t)
        copy = pltpu.make_async_copy(out_ref.at[span, :], out_hbm.at[span, :], sems.at[t])
        copy.start()
        copies.append(copy)
    for copy in copies:
        copy.wait()


def call(kernel, operands, spaces, outs, scratch, flops, name, out_spaces=None, grant=12):
    out_spaces = out_spaces or [VMEM] * len(outs)
    moved = sum(a.size * a.dtype.itemsize for a in operands)
    return pl.pallas_call(
        kernel,
        out_shape=[jax.ShapeDtypeStruct(s, d) for s, d in outs],
        in_specs=[pl.BlockSpec(memory_space=s) for s in spaces],
        out_specs=[pl.BlockSpec(memory_space=s) for s in out_spaces],
        scratch_shapes=scratch,
        compiler_params=pltpu.CompilerParams(vmem_limit_bytes=grant * 1024 * 1024),
        cost_estimate=pl.CostEstimate(flops=flops, bytes_accessed=moved, transcendentals=0),
        name=name,
    )(*operands)


def in_hbm(array):
    return pltpu.with_memory_space_constraint(array, HBM)


def pairings(size, cores):
    opposite = {i: (i + size // 2) % size for i in range(size)}
    ways = [opposite]
    for first in (1, 0):
        way = {}
        for i in range(first, size - 1, 2):
            way[i], way[i + 1] = i + 1, i
        ways.append(way)
    return [
        [
            (i * cores + k, way[i] * cores + k if i in way else i * cores + (k + 1) % cores)
            for i in range(size)
            for k in range(cores)
        ]
        for way in ways
    ]


def exchange(arrays, sizes):
    return [lax.ppermute(a, ("elem", "sub"), p) for a, p in zip(arrays, pairings(*sizes))]


def per_device(
    sizes,
    trace_rhs,
    face_scale,
    stiff_scale,
    mass_scale,
    elem_faces,
    halo_faces,
    elem_count,
    jacobi_block,
    stiffness,
    mass,
    lifting,
):
    faces, width = trace_rhs.shape
    slots = halo_faces.shape[2]
    elems = elem_faces.shape[0]
    face_dofs = jacobi_block.shape[0]
    eld, inside = lifting.shape
    pairs = width // LANES
    halo_rows = LANES
    ext_rows = faces + halo_rows
    slots_all = 6 * elems
    lists = exchange([halo_faces.transpose(1, 0, 2)] * 3, sizes)
    par = (lax.axis_index("elem") % 2).astype(I32).reshape(1)
    stiff_row = stiff_scale.reshape(1, elems)
    mass_row = mass_scale.reshape(1, elems)
    field = ((faces, width), BF16)
    rows = [((slots, width), BF16)] * 3
    x_shape = ((2 * pairs * elems, eld), BF16)
    y_shape = ((slots_all, width), BF16)
    own_shape = ((faces, width), F32)
    element_flops = 4 * 2 * pairs * elems * eld * eld

    step = 4 * face_dofs
    first, block, scale, face_scales, weights = call(
        prepare_kernel,
        [in_hbm(a) for a in (trace_rhs, jacobi_block, face_scale, stiffness, mass)],
        [HBM] * 5,
        [
            field,
            ((step, step), BF16),
            ((1, faces), F32),
            ((faces, LANES), F32),
            ((eld, 2 * eld), BF16),
        ],
        [
            VMEM(*field),
            VMEM(jacobi_block.shape, BF16),
            VMEM(face_scale.shape, F32),
            pltpu.SemaphoreType.DMA((5,)),
        ],
        2 * faces * width * 256,
        "prepare",
    )
    outgoing = call(
        send_kernel,
        [par, first, *lists[::-1]],
        [SMEM] + [VMEM] * 4,
        rows,
        [],
        2 * LANES * faces * width,
        "send",
    )
    arrived = exchange(outgoing, sizes)
    gather_flops = 2 * slots_all * faces * width
    tile = (LANES, LANES)
    own_x, own_pick, halo_pick, spread, element_scales = call(
        functools.partial(first_gather_kernel, slots),
        [par, elem_count, first, elem_faces.T, stiff_row, mass_row],
        [SMEM] * 2 + [VMEM] * 4,
        [
            x_shape,
            ((slots_all, faces), BF16),
            ((slots_all // 2, 2 * halo_rows), BF16),
            ((ext_rows, slots_all), BF16),
            ((2, *tile), F32),
        ],
        [],
        gather_flops,
        "gather1",
    )

    def operator(own_x, arrived, keep_x, name):
        halo = VMEM((2 * halo_rows, 2 * width), BF16)
        return call(
            operator_kernel,
            [halo_pick, spread, own_x, *arrived, element_scales, weights],
            [VMEM] * 8,
            [y_shape, *rows] + ([x_shape] if keep_x else []),
            [halo] if keep_x else [VMEM(*x_shape), halo],
            element_flops,
            name,
        )

    y, *back = operator(own_x, arrived, False, "operator1")
    returned = exchange(back, sizes)
    own, own_rows, same, give, request_scale = call(
        sums_kernel,
        [par, spread, y, *lists[::-1], scale],
        [SMEM] + [VMEM] * 6,
        [
            own_shape,
            ((LANES, width), F32),
            (tile, BF16),
            ((faces, LANES), BF16),
            (tile, F32),
        ],
        [VMEM(*field)] * 2,
        2 * faces * slots_all * width,
        "sums1",
    )
    outgoing = call(
        middle_kernel,
        [own_rows, *returned, same, request_scale, block],
        [VMEM] * 7,
        rows,
        [VMEM((LANES, width), BF16)],
        2 * LANES * width * 256,
        "middle",
    )
    arrived = exchange(outgoing, sizes)
    own_x, lift = call(
        second_gather_kernel,
        [own_pick, own, *returned, give, face_scales, block, in_hbm(lifting)],
        [VMEM] * 8 + [HBM],
        [x_shape, (lifting.shape, BF16)],
        [VMEM((LANES, width), BF16), VMEM(*field), VMEM(*field), pltpu.SemaphoreType.DMA],
        gather_flops,
        "gather2",
    )
    y, *back, x = operator(own_x, arrived, True, "operator2")
    returned = exchange(back, sizes)
    own, interior = call(
        finish_kernel,
        [spread, y, x, lift],
        [VMEM] * 4,
        [own_shape, ((elems, width // face_dofs * inside), BF16)],
        [
            VMEM((elems, width // face_dofs * inside), BF16),
            pltpu.SemaphoreType.DMA((pairs // 2,)),
        ],
        4 * pairs * elems * eld * inside,
        "finish",
        [VMEM, HBM],
    )
    (applied,) = call(
        last_kernel,
        [own, *returned, give],
        [VMEM] * 5,
        [field],
        [
            VMEM((LANES, width), BF16),
            VMEM((faces, width), BF16),
            pltpu.SemaphoreType.DMA((faces // LANES,)),
        ],
        2 * faces * width * 128,
        "last",
        [HBM],
    )
    return (applied, interior)


def solution(mesh):
    rows = P(("grp", "elem", "sub"))
    split = P(("grp", "elem", "sub"), "src")
    in_specs = (
        split,
        rows,
        rows,
        rows,
        P(("grp", "elem", "sub"), None),
        P(("grp", "elem", "sub"), None, None),
        rows,
        P(),
        P(),
        P(),
        P(),
    )
    return jax.shard_map(
        functools.partial(per_device, (mesh.shape["elem"], mesh.shape["sub"])),
        mesh=mesh,
        in_specs=in_specs,
        out_specs=(split, split),
        check_vma=False,
    )
```

```python
import functools

import jax
import jax.numpy as jnp
from jax import lax
from jax.experimental import pallas as pl
from jax.experimental.pallas import tpu as pltpu
from jax.sharding import PartitionSpec as P

F32 = jnp.float32
BF16 = jnp.bfloat16
I32 = jnp.int32
LANES = 128
VMEM = pltpu.VMEM
SMEM = pltpu.SMEM
HBM = pltpu.HBM


def iota(shape, dim):
    return lax.broadcasted_iota(I32, shape, dim)


def one_hot(condition):
    return jnp.where(condition, 1.0, 0.0).astype(BF16)


def matmul(a, b):
    return jnp.dot(a, b, preferred_element_type=F32)


def column_tiles(row):
    count = row.shape[1] // LANES
    return [
        jnp.transpose(
            jnp.broadcast_to(row[:, t * LANES : (t + 1) * LANES].astype(F32), (LANES, LANES))
        )
        for t in range(count)
    ]


def block_diagonal(block, copies):
    rows, cols = block.shape
    wide = jnp.concatenate([block] * copies, axis=1)
    full = jnp.concatenate([wide] * copies, axis=0)
    shape = (rows * copies, cols * copies)
    keep = (iota(shape, 0) // rows) == (iota(shape, 1) // cols)
    return jnp.where(keep, full, jnp.zeros_like(full))


def precondition(field_ref, scale_ref, block_ref, z_ref):
    step = block_ref.shape[0]
    scale = scale_ref[...]
    scale = jnp.concatenate([scale] * (step // LANES), axis=1)
    for start in range(0, field_ref.shape[1], step):
        product = matmul(field_ref[:, start : start + step], block_ref[...])
        z_ref[:, start : start + step] = (product * scale).astype(BF16)


def swap_halves(even, odd, low):
    turn = lambda tile: pltpu.roll(tile, LANES // 2, 1)
    return jnp.where(low, even, turn(odd)), jnp.where(low, turn(even), odd)


def prepare_kernel(
    rhs_hbm, jacobi_hbm, scale_hbm, stiff_hbm, mass_hbm,
    z_ref, block_ref, scale_ref, face_scale_ref, w_ref, rhs_ref, small_ref, line_ref, sems
):
    half = w_ref.shape[1] // 2
    sources = (jacobi_hbm, scale_hbm, rhs_hbm, stiff_hbm, mass_hbm)
    targets = (small_ref, line_ref, rhs_ref, w_ref.at[:, :half], w_ref.at[:, half:])
    copies = [
        pltpu.make_async_copy(src, dst, sems.at[i])
        for i, (src, dst) in enumerate(zip(sources, targets))
    ]
    for copy in copies:
        copy.start()
    copies[0].wait()
    block_ref[...] = block_diagonal(small_ref[...].astype(F32), 4).astype(BF16)
    copies[1].wait()
    scale_ref[...] = line_ref[...].reshape(scale_ref.shape)
    for t, tile in enumerate(column_tiles(scale_ref[...])):
        face_scale_ref[t * LANES : (t + 1) * LANES, :] = tile
    copies[2].wait()
    precondition(rhs_ref, face_scale_ref, block_ref, z_ref)
    copies[3].wait()
    copies[4].wait()


def wanted_part(par, list_ref, colour):
    if colour == 0:
        return list_ref[2]
    return jnp.where(par == 2 - colour, list_ref[0], list_ref[1])


def padded(row):
    return jnp.concatenate([row, jnp.full((1, LANES - row.shape[1]), -1, I32)], axis=1)


def wanted_row(par, list_refs):
    parts = [wanted_part(par, ref, c) for c, ref in enumerate(list_refs)]
    return padded(jnp.concatenate(parts, axis=1))


def wanted_tables(wanted, scale_row):
    (column,) = column_tiles(wanted)
    column = column.astype(I32)
    lane = iota((LANES, LANES), 1)
    picks = []
    scale = jnp.zeros((LANES, LANES), F32)
    for t in range(scale_row.shape[1] // LANES):
        chosen = column == lane + t * LANES
        picks.append(one_hot(chosen))
        across = jnp.broadcast_to(scale_row[:, t * LANES : (t + 1) * LANES], (LANES, LANES))
        scale = scale + jnp.where(chosen, across, 0.0)
    scale = jnp.broadcast_to(jnp.sum(scale, axis=1, keepdims=True), (LANES, LANES))
    return jnp.concatenate(picks, axis=1), scale


def send_rows(rows, scale, block_ref, out_refs):
    step = block_ref.shape[0]
    scale = jnp.concatenate([scale] * (step // LANES), axis=1)
    slots = out_refs[0].shape[0]
    for start in range(0, rows.shape[1], step):
        product = matmul(rows[:, start : start + step], block_ref[...])
        product = (product * scale).astype(BF16)
        for c, ref in enumerate(out_refs):
            ref[:, start : start + step] = product[c * slots : (c + 1) * slots, :]


def send_kernel(par_ref, z_ref, ec_ref, eb_ref, ea_ref, *out_refs):
    (column,) = column_tiles(wanted_row(par_ref[0], [ea_ref, eb_ref, ec_ref]))
    slots = out_refs[0].shape[0]
    column = column[: 3 * slots].astype(I32)
    lane = iota((3 * slots, LANES), 1)
    tiles = range(z_ref.shape[0] // LANES)
    pick = jnp.concatenate([one_hot(column == lane + t * LANES) for t in tiles], axis=1)
    rows = matmul(pick, z_ref[...]).astype(BF16)
    for c, ref in enumerate(out_refs):
        ref[...] = rows[c * slots : (c + 1) * slots, :]


def column_ids(par, faces, slots, tile, axis):
    index = iota((LANES, LANES), axis) + tile * LANES
    moved = jnp.where(index < faces + slots, 2 * slots, slots * par - slots)
    moved = jnp.where(index < faces + 2 * slots, moved, -slots - slots * par)
    return jnp.where(index < faces, index, index + moved)


def element_tables(par, slots, count, ids_ref, own_ref, halo_ref, spread_ref):
    ids_all = jnp.where(iota(ids_ref.shape, 1) < count, ids_ref[...], -1)
    tiles = spread_ref.shape[0] // LANES
    faces = own_ref.shape[1]
    owned = faces // LANES
    lanes = [column_ids(par, faces, slots, t, 1) for t in range(tiles)]
    rows = [column_ids(par, faces, slots, t, 0) for t in range(tiles)]
    span = lambda i: slice(i * LANES, (i + 1) * LANES)
    for k in range(ids_ref.shape[0]):
        across = jnp.broadcast_to(ids_all[k : k + 1, :], (LANES, LANES))
        down = jnp.transpose(across.astype(F32)).astype(I32)
        for t in range(tiles):
            pick = one_hot(down == lanes[t])
            if t < owned:
                own_ref[span(k), span(t)] = pick
            else:
                halo_ref[span(k // 2), span(k % 2)] = pick
            spread_ref[span(t), span(k)] = one_hot(across == rows[t])


def gather_own(pick_ref, z_ref, x_ref):
    width = z_ref.shape[1]
    low = iota((LANES, LANES), 1) < LANES // 2
    for t in range(x_ref.shape[1] // LANES):
        rows = matmul(pick_ref[2 * t * LANES : 2 * (t + 1) * LANES, :], z_ref[...])
        for p in range(width // LANES):
            pair = rows[:, p * LANES : (p + 1) * LANES]
            even, odd = swap_halves(pair[:LANES], pair[LANES:], low)
            at = 2 * p * LANES
            x_ref[at : at + LANES, t * LANES : (t + 1) * LANES] = even.astype(BF16)
            x_ref[at + LANES : at + 2 * LANES, t * LANES : (t + 1) * LANES] = odd.astype(BF16)


def first_gather_kernel(
    slots, par_ref, count_ref, z_ref, ids_ref, stiff_scale_ref, mass_scale_ref,
    x_ref, own_ref, halo_ref, spread_ref, element_scale_ref
):
    element_tables(par_ref[0], slots, count_ref[0], ids_ref, own_ref, halo_ref, spread_ref)
    gather_own(own_ref, z_ref, x_ref)
    (element_scale_ref[0],) = column_tiles(stiff_scale_ref[...])
    (element_scale_ref[1],) = column_tiles(mass_scale_ref[...])


def second_gather_kernel(
    pick_ref, sums_ref, ba_ref, bb_ref, bc_ref, give_ref, scale_ref, block_ref, lift_hbm,
    x_ref, lift_ref, gathered_ref, v_ref, z_ref, sem
):
    load = pltpu.make_async_copy(lift_hbm, lift_ref, sem)
    load.start()
    gather_back([ba_ref, bb_ref, bc_ref], gathered_ref)
    for t in range(sums_ref.shape[0] // LANES):
        v_ref[t * LANES : (t + 1) * LANES, :] = collected(sums_ref, give_ref, gathered_ref, t)
    precondition(v_ref, scale_ref, block_ref, z_ref)
    gather_own(pick_ref, z_ref, x_ref)
    load.wait()


def operator_kernel(
    pick_ref, spread_ref, own_x_ref, aa_ref, ab_ref, ac_ref, scale_ref,
    w_ref, y_ref, ba_ref, bb_ref, bc_ref, x_ref, halo_ref
):
    slots, width = aa_ref.shape
    pairs = width // LANES
    filled = 3 * slots
    arrived = jnp.concatenate([aa_ref[...], ab_ref[...], ac_ref[...]], axis=0).astype(F32)
    low = iota((filled, LANES), 1) < LANES // 2
    zero = jnp.zeros((filled, LANES), F32)
    for first in (0, LANES):
        halo_ref[first + filled : first + LANES, :] = jnp.zeros(
            (LANES - filled, halo_ref.shape[1]), BF16
        )
    for p in range(pairs):
        tile = arrived[:, p * LANES : (p + 1) * LANES]
        turned = pltpu.roll(tile, LANES // 2, 1)
        even = slice(2 * p * LANES, (2 * p + 1) * LANES)
        odd = slice((2 * p + 1) * LANES, (2 * p + 2) * LANES)
        halo_ref[:filled, even] = jnp.where(low, tile, zero).astype(BF16)
        halo_ref[LANES : LANES + filled, even] = jnp.where(low, zero, turned).astype(BF16)
        halo_ref[:filled, odd] = jnp.where(low, turned, zero).astype(BF16)
        halo_ref[LANES : LANES + filled, odd] = jnp.where(low, zero, tile).astype(BF16)
    for t in range(x_ref.shape[1] // LANES):
        rows = matmul(pick_ref[t * LANES : (t + 1) * LANES, :], halo_ref[...]).astype(BF16)
        for s in range(2 * pairs):
            at = (slice(s * LANES, (s + 1) * LANES), slice(t * LANES, (t + 1) * LANES))
            x_ref[at] = own_x_ref[at] + rows[:, s * LANES : (s + 1) * LANES]
    stiff = jnp.concatenate([scale_ref[0]] * 2, axis=0)
    mass = jnp.concatenate([scale_ref[1]] * 2, axis=0)
    low = iota((LANES, LANES), 1) < LANES // 2
    half = w_ref.shape[1] // 2
    for p in range(pairs):
        product = matmul(x_ref[2 * p * LANES : 2 * (p + 1) * LANES, :], w_ref[...])
        for t in range(half // LANES):
            at = t * LANES
            term = (
                stiff * product[:, at : at + LANES]
                - mass * product[:, half + at : half + at + LANES]
            )
            first, second = swap_halves(term[:LANES], term[LANES:], low)
            place = slice(p * LANES, (p + 1) * LANES)
            y_ref[2 * at : 2 * at + LANES, place] = first.astype(BF16)
            y_ref[2 * at + LANES : 2 * at + 2 * LANES, place] = second.astype(BF16)
    faces = spread_ref.shape[0] - LANES
    rows = matmul(spread_ref[faces : faces + filled, :], y_ref[...]).astype(BF16)
    for c, ref in enumerate((ba_ref, bb_ref, bc_ref)):
        ref[...] = rows[c * slots : (c + 1) * slots, :]


def own_sums(spread_ref, y_ref, own_ref):
    for t in range(own_ref.shape[0] // LANES):
        own_ref[t * LANES : (t + 1) * LANES, :] = matmul(
            spread_ref[t * LANES : (t + 1) * LANES, :], y_ref[...]
        )


def sums_kernel(
    par_ref, spread_ref, y_ref, ec_ref, eb_ref, ea_ref, scale_ref,
    own_ref, rows_ref, same_ref, give_ref, request_scale_ref, high_ref, low_ref
):
    wanted = wanted_row(par_ref[0], [ea_ref, eb_ref, ec_ref])
    request, request_scale_ref[...] = wanted_tables(wanted, scale_ref[...])
    target = jnp.broadcast_to(wanted, give_ref.shape)
    give_ref[...] = one_hot(target == iota(give_ref.shape, 0))
    own_sums(spread_ref, y_ref, own_ref)
    same_ref[...] = matmul(request, give_ref[...]).astype(BF16)
    high_ref[...] = own_ref[...].astype(BF16)
    low_ref[...] = (own_ref[...] - high_ref[...].astype(F32)).astype(BF16)
    rows_ref[...] = matmul(request, high_ref[...])
    rows_ref[...] += matmul(request, low_ref[...])


def finish_kernel(
    spread_ref, y_ref, x_ref, lift_ref, own_ref, interior_hbm, inside_ref, sems
):
    wide = lift_ref.shape[1]
    step = 4
    copies = []
    for start in range(0, x_ref.shape[0] // LANES, step):
        rows = x_ref[start * LANES : (start + step) * LANES, :]
        product = matmul(rows, lift_ref[...]).astype(BF16)
        for r in range(step):
            inside_ref[:, (start + r) * wide : (start + r + 1) * wide] = product[
                r * LANES : (r + 1) * LANES, :
            ]
        span = pl.ds(start * wide, step * wide)
        copy = pltpu.make_async_copy(
            inside_ref.at[:, span], interior_hbm.at[:, span], sems.at[len(copies)]
        )
        copy.start()
        copies.append(copy)
    own_sums(spread_ref, y_ref, own_ref)
    for copy in copies:
        copy.wait()


def gather_back(back_refs, gathered_ref):
    slots, width = back_refs[0].shape
    for c, ref in enumerate(back_refs):
        gathered_ref[c * slots : (c + 1) * slots, :] = ref[...]
    gathered_ref[3 * slots :, :] = jnp.zeros((LANES - 3 * slots, width), BF16)


def collected(own_ref, give_ref, gathered_ref, tile):
    rows = slice(tile * LANES, (tile + 1) * LANES)
    return (own_ref[rows, :] + matmul(give_ref[rows, :], gathered_ref[...])).astype(BF16)


def middle_kernel(
    rows_ref, ba_ref, bb_ref, bc_ref, same_ref, request_scale_ref, block_ref,
    oa_ref, ob_ref, oc_ref, gathered_ref
):
    gather_back([ba_ref, bb_ref, bc_ref], gathered_ref)
    count = 3 * oa_ref.shape[0]
    rows = rows_ref[:count, :] + matmul(same_ref[:count, :], gathered_ref[...])
    send_rows(rows.astype(BF16), request_scale_ref[:count, :], block_ref, [oa_ref, ob_ref, oc_ref])


def last_kernel(
    own_ref, ba_ref, bb_ref, bc_ref, give_ref, out_hbm, gathered_ref, out_ref, sems
):
    gather_back([ba_ref, bb_ref, bc_ref], gathered_ref)
    copies = []
    for t in range(own_ref.shape[0] // LANES):
        span = pl.ds(t * LANES, LANES)
        out_ref[span, :] = collected(own_ref, give_ref, gathered_ref, t)
        copy = pltpu.make_async_copy(out_ref.at[span, :], out_hbm.at[span, :], sems.at[t])
        copy.start()
        copies.append(copy)
    for copy in copies:
        copy.wait()


def call(kernel, operands, spaces, outs, scratch, flops, name, out_spaces=None, grant=12):
    out_spaces = out_spaces or [VMEM] * len(outs)
    moved = sum(a.size * a.dtype.itemsize for a in operands)
    return pl.pallas_call(
        kernel,
        out_shape=[jax.ShapeDtypeStruct(s, d) for s, d in outs],
        in_specs=[pl.BlockSpec(memory_space=s) for s in spaces],
        out_specs=[pl.BlockSpec(memory_space=s) for s in out_spaces],
        scratch_shapes=scratch,
        compiler_params=pltpu.CompilerParams(vmem_limit_bytes=grant * 1024 * 1024),
        cost_estimate=pl.CostEstimate(flops=flops, bytes_accessed=moved, transcendentals=0),
        name=name,
    )(*operands)


def in_hbm(array):
    return pltpu.with_memory_space_constraint(array, HBM)


def pairings(size, cores):
    opposite = {i: (i + size // 2) % size for i in range(size)}
    ways = [opposite]
    for first in (1, 0):
        way = {}
        for i in range(first, size - 1, 2):
            way[i], way[i + 1] = i + 1, i
        ways.append(way)
    return [
        [
            (i * cores + k, way[i] * cores + k if i in way else i * cores + (k + 1) % cores)
            for i in range(size)
            for k in range(cores)
        ]
        for way in ways
    ]


def exchange(arrays, sizes):
    return [lax.ppermute(a, ("elem", "sub"), p) for a, p in zip(arrays, pairings(*sizes))]


def per_device(
    sizes,
    trace_rhs,
    face_scale,
    stiff_scale,
    mass_scale,
    elem_faces,
    halo_faces,
    elem_count,
    jacobi_block,
    stiffness,
    mass,
    lifting,
):
    faces, width = trace_rhs.shape
    slots = halo_faces.shape[2]
    elems = elem_faces.shape[0]
    face_dofs = jacobi_block.shape[0]
    eld, inside = lifting.shape
    pairs = width // LANES
    halo_rows = LANES
    ext_rows = faces + halo_rows
    slots_all = 6 * elems
    lists = exchange([halo_faces.transpose(1, 0, 2)] * 3, sizes)
    par = (lax.axis_index("elem") % 2).astype(I32).reshape(1)
    stiff_row = stiff_scale.reshape(1, elems)
    mass_row = mass_scale.reshape(1, elems)
    field = ((faces, width), BF16)
    rows = [((slots, width), BF16)] * 3
    x_shape = ((2 * pairs * elems, eld), BF16)
    y_shape = ((slots_all, width), BF16)
    own_shape = ((faces, width), F32)
    element_flops = 4 * 2 * pairs * elems * eld * eld

    step = 4 * face_dofs
    first, block, scale, face_scales, weights = call(
        prepare_kernel,
        [in_hbm(a) for a in (trace_rhs, jacobi_block, face_scale, stiffness, mass)],
        [HBM] * 5,
        [
            field,
            ((step, step), BF16),
            ((1, faces), F32),
            ((faces, LANES), F32),
            ((eld, 2 * eld), BF16),
        ],
        [
            VMEM(*field),
            VMEM(jacobi_block.shape, BF16),
            VMEM(face_scale.shape, F32),
            pltpu.SemaphoreType.DMA((5,)),
        ],
        2 * faces * width * 256,
        "prepare",
    )
    outgoing = call(
        send_kernel,
        [par, first, *lists[::-1]],
        [SMEM] + [VMEM] * 4,
        rows,
        [],
        2 * LANES * faces * width,
        "send",
    )
    arrived = exchange(outgoing, sizes)
    gather_flops = 2 * slots_all * faces * width
    tile = (LANES, LANES)
    own_x, own_pick, halo_pick, spread, element_scales = call(
        functools.partial(first_gather_kernel, slots),
        [par, elem_count, first, elem_faces.T, stiff_row, mass_row],
        [SMEM] * 2 + [VMEM] * 4,
        [
            x_shape,
            ((slots_all, faces), BF16),
            ((slots_all // 2, 2 * halo_rows), BF16),
            ((ext_rows, slots_all), BF16),
            ((2, *tile), F32),
        ],
        [],
        gather_flops,
        "gather1",
    )

    def operator(own_x, arrived, keep_x, name):
        halo = VMEM((2 * halo_rows, 2 * width), BF16)
        return call(
            operator_kernel,
            [halo_pick, spread, own_x, *arrived, element_scales, weights],
            [VMEM] * 8,
            [y_shape, *rows] + ([x_shape] if keep_x else []),
            [halo] if keep_x else [VMEM(*x_shape), halo],
            element_flops,
            name,
        )

    y, *back = operator(own_x, arrived, False, "operator1")
    returned = exchange(back, sizes)
    own, own_rows, same, give, request_scale = call(
        sums_kernel,
        [par, spread, y, *lists[::-1], scale],
        [SMEM] + [VMEM] * 6,
        [
            own_shape,
            ((LANES, width), F32),
            (tile, BF16),
            ((faces, LANES), BF16),
            (tile, F32),
        ],
        [VMEM(*field)] * 2,
        2 * faces * slots_all * width,
        "sums1",
    )
    outgoing = call(
        middle_kernel,
        [own_rows, *returned, same, request_scale, block],
        [VMEM] * 7,
        rows,
        [VMEM((LANES, width), BF16)],
        2 * LANES * width * 256,
        "middle",
    )
    arrived = exchange(outgoing, sizes)
    own_x, lift = call(
        second_gather_kernel,
        [own_pick, own, *returned, give, face_scales, block, in_hbm(lifting)],
        [VMEM] * 8 + [HBM],
        [x_shape, (lifting.shape, BF16)],
        [VMEM((LANES, width), BF16), VMEM(*field), VMEM(*field), pltpu.SemaphoreType.DMA],
        gather_flops,
        "gather2",
    )
    y, *back, x = operator(own_x, arrived, True, "operator2")
    returned = exchange(back, sizes)
    own, interior = call(
        finish_kernel,
        [spread, y, x, lift],
        [VMEM] * 4,
        [own_shape, ((elems, width // face_dofs * inside), BF16)],
        [
            VMEM((elems, width // face_dofs * inside), BF16),
            pltpu.SemaphoreType.DMA((pairs // 2,)),
        ],
        4 * pairs * elems * eld * inside,
        "finish",
        [VMEM, HBM],
    )
    (applied,) = call(
        last_kernel,
        [own, *returned, give],
        [VMEM] * 5,
        [field],
        [
            VMEM((LANES, width), BF16),
            VMEM((faces, width), BF16),
            pltpu.SemaphoreType.DMA((faces // LANES,)),
        ],
        2 * faces * width * 128,
        "last",
        [HBM],
    )
    return (applied, interior)


def solution(mesh):
    rows = P(("grp", "elem", "sub"))
    split = P(("grp", "elem", "sub"), "src")
    in_specs = (
        split,
        rows,
        rows,
        rows,
        P(("grp", "elem", "sub"), None),
        P(("grp", "elem", "sub"), None, None),
        rows,
        P(),
        P(),
        P(),
        P(),
    )
    return jax.shard_map(
        functools.partial(per_device, (mesh.shape["elem"], mesh.shape["sub"])),
        mesh=mesh,
        in_specs=in_specs,
        out_specs=(split, split),
        check_vma=False,
    )
```

```python
import functools

import jax
import jax.numpy as jnp
from jax import lax
from jax.experimental import pallas as pl
from jax.experimental.pallas import tpu as pltpu
from jax.sharding import PartitionSpec as P

F32 = jnp.float32
BF16 = jnp.bfloat16
I32 = jnp.int32
LANES = 128
VMEM = pltpu.VMEM
SMEM = pltpu.SMEM
HBM = pltpu.HBM


def iota(shape, dim):
    return lax.broadcasted_iota(I32, shape, dim)


def one_hot(condition):
    return jnp.where(condition, 1.0, 0.0).astype(BF16)


def matmul(a, b):
    return jnp.dot(a, b, preferred_element_type=F32)


def column_tiles(row):
    count = row.shape[1] // LANES
    return [
        jnp.transpose(
            jnp.broadcast_to(row[:, t * LANES : (t + 1) * LANES].astype(F32), (LANES, LANES))
        )
        for t in range(count)
    ]


def block_diagonal(block, copies):
    rows, cols = block.shape
    wide = jnp.concatenate([block] * copies, axis=1)
    full = jnp.concatenate([wide] * copies, axis=0)
    shape = (rows * copies, cols * copies)
    keep = (iota(shape, 0) // rows) == (iota(shape, 1) // cols)
    return jnp.where(keep, full, jnp.zeros_like(full))


def precondition(field_ref, scale_ref, block_ref, z_ref):
    step = block_ref.shape[0]
    scale = scale_ref[...]
    scale = jnp.concatenate([scale] * (step // LANES), axis=1)
    for start in range(0, field_ref.shape[1], step):
        product = matmul(field_ref[:, start : start + step], block_ref[...])
        z_ref[:, start : start + step] = (product * scale).astype(BF16)


def swap_halves(even, odd, low):
    turn = lambda tile: pltpu.roll(tile, LANES // 2, 1)
    return jnp.where(low, even, turn(odd)), jnp.where(low, turn(even), odd)


def prepare_kernel(
    rhs_hbm, jacobi_hbm, scale_hbm, stiff_hbm, mass_hbm,
    z_ref, block_ref, scale_ref, face_scale_ref, w_ref, rhs_ref, small_ref, line_ref, sems
):
    half = w_ref.shape[1] // 2
    sources = (jacobi_hbm, scale_hbm, rhs_hbm, stiff_hbm, mass_hbm)
    targets = (small_ref, line_ref, rhs_ref, w_ref.at[:, :half], w_ref.at[:, half:])
    copies = [
        pltpu.make_async_copy(src, dst, sems.at[i])
        for i, (src, dst) in enumerate(zip(sources, targets))
    ]
    for copy in copies:
        copy.start()
    copies[0].wait()
    block_ref[...] = block_diagonal(small_ref[...].astype(F32), 4).astype(BF16)
    copies[1].wait()
    scale_ref[...] = line_ref[...].reshape(scale_ref.shape)
    for t, tile in enumerate(column_tiles(scale_ref[...])):
        face_scale_ref[t * LANES : (t + 1) * LANES, :] = tile
    copies[2].wait()
    precondition(rhs_ref, face_scale_ref, block_ref, z_ref)
    copies[3].wait()
    copies[4].wait()


def wanted_part(par, list_ref, colour):
    if colour == 0:
        return list_ref[2]
    return jnp.where(par == 2 - colour, list_ref[0], list_ref[1])


def padded(row):
    return jnp.concatenate([row, jnp.full((1, LANES - row.shape[1]), -1, I32)], axis=1)


def wanted_row(par, list_refs):
    parts = [wanted_part(par, ref, c) for c, ref in enumerate(list_refs)]
    return padded(jnp.concatenate(parts, axis=1))


def wanted_tables(wanted, scale_row):
    (column,) = column_tiles(wanted)
    column = column.astype(I32)
    lane = iota((LANES, LANES), 1)
    picks = []
    scale = jnp.zeros((LANES, LANES), F32)
    for t in range(scale_row.shape[1] // LANES):
        chosen = column == lane + t * LANES
        picks.append(one_hot(chosen))
        across = jnp.broadcast_to(scale_row[:, t * LANES : (t + 1) * LANES], (LANES, LANES))
        scale = scale + jnp.where(chosen, across, 0.0)
    scale = jnp.broadcast_to(jnp.sum(scale, axis=1, keepdims=True), (LANES, LANES))
    return jnp.concatenate(picks, axis=1), scale


def send_rows(rows, scale, block_ref, out_refs):
    step = block_ref.shape[0]
    scale = jnp.concatenate([scale] * (step // LANES), axis=1)
    slots = out_refs[0].shape[0]
    for start in range(0, rows.shape[1], step):
        product = matmul(rows[:, start : start + step], block_ref[...])
        product = (product * scale).astype(BF16)
        for c, ref in enumerate(out_refs):
            ref[:, start : start + step] = product[c * slots : (c + 1) * slots, :]


def send_kernel(par_ref, z_ref, ec_ref, eb_ref, ea_ref, *out_refs):
    (column,) = column_tiles(wanted_row(par_ref[0], [ea_ref, eb_ref, ec_ref]))
    column = column.astype(I32)
    lane = iota((LANES, LANES), 1)
    tiles = range(z_ref.shape[0] // LANES)
    pick = jnp.concatenate([one_hot(column == lane + t * LANES) for t in tiles], axis=1)
    rows = matmul(pick, z_ref[...]).astype(BF16)
    slots = out_refs[0].shape[0]
    for c, ref in enumerate(out_refs):
        ref[...] = rows[c * slots : (c + 1) * slots, :]


def column_ids(par, faces, slots, tile, axis):
    index = iota((LANES, LANES), axis) + tile * LANES
    moved = jnp.where(index < faces + slots, 2 * slots, slots * par - slots)
    moved = jnp.where(index < faces + 2 * slots, moved, -slots - slots * par)
    return jnp.where(index < faces, index, index + moved)


def element_tables(par, slots, count, ids_ref, own_ref, halo_ref, spread_ref):
    ids_all = jnp.where(iota(ids_ref.shape, 1) < count, ids_ref[...], -1)
    tiles = spread_ref.shape[0] // LANES
    faces = own_ref.shape[1]
    owned = faces // LANES
    lanes = [column_ids(par, faces, slots, t, 1) for t in range(tiles)]
    rows = [column_ids(par, faces, slots, t, 0) for t in range(tiles)]
    span = lambda i: slice(i * LANES, (i + 1) * LANES)
    for k in range(ids_ref.shape[0]):
        across = jnp.broadcast_to(ids_all[k : k + 1, :], (LANES, LANES))
        down = jnp.transpose(across.astype(F32)).astype(I32)
        for t in range(tiles):
            pick = one_hot(down == lanes[t])
            if t < owned:
                own_ref[span(k), span(t)] = pick
            else:
                halo_ref[span(k // 2), span(k % 2)] = pick
            spread_ref[span(t), span(k)] = one_hot(across == rows[t])


def gather_own(pick_ref, z_ref, x_ref):
    width = z_ref.shape[1]
    low = iota((LANES, LANES), 1) < LANES // 2
    for t in range(x_ref.shape[1] // LANES):
        rows = matmul(pick_ref[2 * t * LANES : 2 * (t + 1) * LANES, :], z_ref[...])
        for p in range(width // LANES):
            pair = rows[:, p * LANES : (p + 1) * LANES]
            even, odd = swap_halves(pair[:LANES], pair[LANES:], low)
            at = 2 * p * LANES
            x_ref[at : at + LANES, t * LANES : (t + 1) * LANES] = even.astype(BF16)
            x_ref[at + LANES : at + 2 * LANES, t * LANES : (t + 1) * LANES] = odd.astype(BF16)


def first_gather_kernel(
    slots, par_ref, count_ref, z_ref, ids_ref, stiff_scale_ref, mass_scale_ref,
    x_ref, own_ref, halo_ref, spread_ref, element_scale_ref
):
    element_tables(par_ref[0], slots, count_ref[0], ids_ref, own_ref, halo_ref, spread_ref)
    gather_own(own_ref, z_ref, x_ref)
    (element_scale_ref[0],) = column_tiles(stiff_scale_ref[...])
    (element_scale_ref[1],) = column_tiles(mass_scale_ref[...])


def second_gather_kernel(
    pick_ref, sums_ref, ba_ref, bb_ref, bc_ref, give_ref, scale_ref, block_ref, lift_hbm,
    x_ref, lift_ref, gathered_ref, v_ref, z_ref, sem
):
    load = pltpu.make_async_copy(lift_hbm, lift_ref, sem)
    load.start()
    gather_back([ba_ref, bb_ref, bc_ref], gathered_ref)
    for t in range(sums_ref.shape[0] // LANES):
        v_ref[t * LANES : (t + 1) * LANES, :] = collected(sums_ref, give_ref, gathered_ref, t)
    precondition(v_ref, scale_ref, block_ref, z_ref)
    gather_own(pick_ref, z_ref, x_ref)
    load.wait()


def operator_kernel(
    pick_ref, spread_ref, own_x_ref, aa_ref, ab_ref, ac_ref, scale_ref,
    w_ref, y_ref, ba_ref, bb_ref, bc_ref, x_ref, halo_ref
):
    slots, width = aa_ref.shape
    pairs = width // LANES
    filled = 3 * slots
    arrived = jnp.concatenate([aa_ref[...], ab_ref[...], ac_ref[...]], axis=0)
    low = iota((filled, LANES), 1) < LANES // 2
    zero = jnp.zeros((filled, LANES), BF16)
    for first in (0, LANES):
        halo_ref[first + filled : first + LANES, :] = jnp.zeros(
            (LANES - filled, halo_ref.shape[1]), BF16
        )
    for p in range(pairs):
        tile = arrived[:, p * LANES : (p + 1) * LANES]
        turned = pltpu.roll(tile, LANES // 2, 1)
        even = slice(2 * p * LANES, (2 * p + 1) * LANES)
        odd = slice((2 * p + 1) * LANES, (2 * p + 2) * LANES)
        halo_ref[:filled, even] = jnp.where(low, tile, zero)
        halo_ref[LANES : LANES + filled, even] = jnp.where(low, zero, turned)
        halo_ref[:filled, odd] = jnp.where(low, turned, zero)
        halo_ref[LANES : LANES + filled, odd] = jnp.where(low, zero, tile)
    for t in range(x_ref.shape[1] // LANES):
        rows = matmul(pick_ref[t * LANES : (t + 1) * LANES, :], halo_ref[...]).astype(BF16)
        for s in range(2 * pairs):
            at = (slice(s * LANES, (s + 1) * LANES), slice(t * LANES, (t + 1) * LANES))
            x_ref[at] = own_x_ref[at] + rows[:, s * LANES : (s + 1) * LANES]
    stiff = jnp.concatenate([scale_ref[0]] * 2, axis=0)
    mass = jnp.concatenate([scale_ref[1]] * 2, axis=0)
    low = iota((LANES, LANES), 1) < LANES // 2
    half = w_ref.shape[1] // 2
    for p in range(pairs):
        product = matmul(x_ref[2 * p * LANES : 2 * (p + 1) * LANES, :], w_ref[...])
        for t in range(half // LANES):
            at = t * LANES
            term = (
                stiff * product[:, at : at + LANES]
                - mass * product[:, half + at : half + at + LANES]
            )
            first, second = swap_halves(term[:LANES], term[LANES:], low)
            place = slice(p * LANES, (p + 1) * LANES)
            y_ref[2 * at : 2 * at + LANES, place] = first.astype(BF16)
            y_ref[2 * at + LANES : 2 * at + 2 * LANES, place] = second.astype(BF16)
    rows = matmul(spread_ref[spread_ref.shape[0] - LANES :, :], y_ref[...]).astype(BF16)
    for c, ref in enumerate((ba_ref, bb_ref, bc_ref)):
        ref[...] = rows[c * slots : (c + 1) * slots, :]


def own_sums(spread_ref, y_ref, own_ref):
    for t in range(own_ref.shape[0] // LANES):
        own_ref[t * LANES : (t + 1) * LANES, :] = matmul(
            spread_ref[t * LANES : (t + 1) * LANES, :], y_ref[...]
        )


def sums_kernel(
    par_ref, spread_ref, y_ref, ec_ref, eb_ref, ea_ref, scale_ref,
    own_ref, rows_ref, same_ref, give_ref, request_scale_ref, high_ref, low_ref
):
    wanted = wanted_row(par_ref[0], [ea_ref, eb_ref, ec_ref])
    request, request_scale_ref[...] = wanted_tables(wanted, scale_ref[...])
    target = jnp.broadcast_to(wanted, give_ref.shape)
    give_ref[...] = one_hot(target == iota(give_ref.shape, 0))
    own_sums(spread_ref, y_ref, own_ref)
    same_ref[...] = matmul(request, give_ref[...]).astype(BF16)
    high_ref[...] = own_ref[...].astype(BF16)
    low_ref[...] = (own_ref[...] - high_ref[...].astype(F32)).astype(BF16)
    rows_ref[...] = matmul(request, high_ref[...])
    rows_ref[...] += matmul(request, low_ref[...])


def finish_kernel(
    spread_ref, y_ref, x_ref, lift_ref, own_ref, interior_hbm, inside_ref, sems
):
    wide = lift_ref.shape[1]
    step = 4
    copies = []
    for start in range(0, x_ref.shape[0] // LANES, step):
        rows = x_ref[start * LANES : (start + step) * LANES, :]
        product = matmul(rows, lift_ref[...]).astype(BF16)
        for r in range(step):
            inside_ref[:, (start + r) * wide : (start + r + 1) * wide] = product[
                r * LANES : (r + 1) * LANES, :
            ]
        span = pl.ds(start * wide, step * wide)
        copy = pltpu.make_async_copy(
            inside_ref.at[:, span], interior_hbm.at[:, span], sems.at[len(copies)]
        )
        copy.start()
        copies.append(copy)
    own_sums(spread_ref, y_ref, own_ref)
    for copy in copies:
        copy.wait()


def gather_back(back_refs, gathered_ref):
    slots, width = back_refs[0].shape
    for c, ref in enumerate(back_refs):
        gathered_ref[c * slots : (c + 1) * slots, :] = ref[...]
    gathered_ref[3 * slots :, :] = jnp.zeros((LANES - 3 * slots, width), BF16)


def collected(own_ref, give_ref, gathered_ref, tile):
    rows = slice(tile * LANES, (tile + 1) * LANES)
    return (own_ref[rows, :] + matmul(give_ref[rows, :], gathered_ref[...])).astype(BF16)


def middle_kernel(
    rows_ref, ba_ref, bb_ref, bc_ref, same_ref, request_scale_ref, block_ref,
    oa_ref, ob_ref, oc_ref, gathered_ref
):
    gather_back([ba_ref, bb_ref, bc_ref], gathered_ref)
    rows = (rows_ref[...] + matmul(same_ref[...], gathered_ref[...])).astype(BF16)
    send_rows(rows, request_scale_ref[...], block_ref, [oa_ref, ob_ref, oc_ref])


def last_kernel(
    own_ref, ba_ref, bb_ref, bc_ref, give_ref, out_hbm, gathered_ref, out_ref, sems
):
    gather_back([ba_ref, bb_ref, bc_ref], gathered_ref)
    copies = []
    for t in range(own_ref.shape[0] // LANES):
        span = pl.ds(t * LANES, LANES)
        out_ref[span, :] = collected(own_ref, give_ref, gathered_ref, t)
        copy = pltpu.make_async_copy(out_ref.at[span, :], out_hbm.at[span, :], sems.at[t])
        copy.start()
        copies.append(copy)
    for copy in copies:
        copy.wait()


def call(kernel, operands, spaces, outs, scratch, flops, name, out_spaces=None, grant=12):
    out_spaces = out_spaces or [VMEM] * len(outs)
    moved = sum(a.size * a.dtype.itemsize for a in operands)
    return pl.pallas_call(
        kernel,
        out_shape=[jax.ShapeDtypeStruct(s, d) for s, d in outs],
        in_specs=[pl.BlockSpec(memory_space=s) for s in spaces],
        out_specs=[pl.BlockSpec(memory_space=s) for s in out_spaces],
        scratch_shapes=scratch,
        compiler_params=pltpu.CompilerParams(vmem_limit_bytes=grant * 1024 * 1024),
        cost_estimate=pl.CostEstimate(flops=flops, bytes_accessed=moved, transcendentals=0),
        name=name,
    )(*operands)


def in_hbm(array):
    return pltpu.with_memory_space_constraint(array, HBM)


def pairings(size, cores):
    opposite = {i: (i + size // 2) % size for i in range(size)}
    ways = [opposite]
    for first in (1, 0):
        way = {}
        for i in range(first, size - 1, 2):
            way[i], way[i + 1] = i + 1, i
        ways.append(way)
    return [
        [
            (i * cores + k, way[i] * cores + k if i in way else i * cores + (k + 1) % cores)
            for i in range(size)
            for k in range(cores)
        ]
        for way in ways
    ]


def exchange(arrays, sizes):
    return [lax.ppermute(a, ("elem", "sub"), p) for a, p in zip(arrays, pairings(*sizes))]


def per_device(
    sizes,
    trace_rhs,
    face_scale,
    stiff_scale,
    mass_scale,
    elem_faces,
    halo_faces,
    elem_count,
    jacobi_block,
    stiffness,
    mass,
    lifting,
):
    faces, width = trace_rhs.shape
    slots = halo_faces.shape[2]
    elems = elem_faces.shape[0]
    face_dofs = jacobi_block.shape[0]
    eld, inside = lifting.shape
    pairs = width // LANES
    halo_rows = LANES
    ext_rows = faces + halo_rows
    slots_all = 6 * elems
    lists = exchange([halo_faces.transpose(1, 0, 2)] * 3, sizes)
    par = (lax.axis_index("elem") % 2).astype(I32).reshape(1)
    stiff_row = stiff_scale.reshape(1, elems)
    mass_row = mass_scale.reshape(1, elems)
    field = ((faces, width), BF16)
    rows = [((slots, width), BF16)] * 3
    x_shape = ((2 * pairs * elems, eld), BF16)
    y_shape = ((slots_all, width), BF16)
    own_shape = ((faces, width), F32)
    element_flops = 4 * 2 * pairs * elems * eld * eld

    step = 4 * face_dofs
    first, block, scale, face_scales, weights = call(
        prepare_kernel,
        [in_hbm(a) for a in (trace_rhs, jacobi_block, face_scale, stiffness, mass)],
        [HBM] * 5,
        [
            field,
            ((step, step), BF16),
            ((1, faces), F32),
            ((faces, LANES), F32),
            ((eld, 2 * eld), BF16),
        ],
        [
            VMEM(*field),
            VMEM(jacobi_block.shape, BF16),
            VMEM(face_scale.shape, F32),
            pltpu.SemaphoreType.DMA((5,)),
        ],
        2 * faces * width * 256,
        "prepare",
    )
    outgoing = call(
        send_kernel,
        [par, first, *lists[::-1]],
        [SMEM] + [VMEM] * 4,
        rows,
        [],
        2 * LANES * faces * width,
        "send",
    )
    arrived = exchange(outgoing, sizes)
    gather_flops = 2 * slots_all * faces * width
    tile = (LANES, LANES)
    own_x, own_pick, halo_pick, spread, element_scales = call(
        functools.partial(first_gather_kernel, slots),
        [par, elem_count, first, elem_faces.T, stiff_row, mass_row],
        [SMEM] * 2 + [VMEM] * 4,
        [
            x_shape,
            ((slots_all, faces), BF16),
            ((slots_all // 2, 2 * halo_rows), BF16),
            ((ext_rows, slots_all), BF16),
            ((2, *tile), F32),
        ],
        [],
        gather_flops,
        "gather1",
    )

    def operator(own_x, arrived, keep_x, name):
        halo = VMEM((2 * halo_rows, 2 * width), BF16)
        return call(
            operator_kernel,
            [halo_pick, spread, own_x, *arrived, element_scales, weights],
            [VMEM] * 8,
            [y_shape, *rows] + ([x_shape] if keep_x else []),
            [halo] if keep_x else [VMEM(*x_shape), halo],
            element_flops,
            name,
        )

    y, *back = operator(own_x, arrived, False, "operator1")
    returned = exchange(back, sizes)
    own, own_rows, same, give, request_scale = call(
        sums_kernel,
        [par, spread, y, *lists[::-1], scale],
        [SMEM] + [VMEM] * 6,
        [
            own_shape,
            ((LANES, width), F32),
            (tile, BF16),
            ((faces, LANES), BF16),
            (tile, F32),
        ],
        [VMEM(*field)] * 2,
        2 * faces * slots_all * width,
        "sums1",
    )
    outgoing = call(
        middle_kernel,
        [own_rows, *returned, same, request_scale, block],
        [VMEM] * 7,
        rows,
        [VMEM((LANES, width), BF16)],
        2 * LANES * width * 256,
        "middle",
    )
    arrived = exchange(outgoing, sizes)
    own_x, lift = call(
        second_gather_kernel,
        [own_pick, own, *returned, give, face_scales, block, in_hbm(lifting)],
        [VMEM] * 8 + [HBM],
        [x_shape, (lifting.shape, BF16)],
        [VMEM((LANES, width), BF16), VMEM(*field), VMEM(*field), pltpu.SemaphoreType.DMA],
        gather_flops,
        "gather2",
    )
    y, *back, x = operator(own_x, arrived, True, "operator2")
    returned = exchange(back, sizes)
    own, interior = call(
        finish_kernel,
        [spread, y, x, lift],
        [VMEM] * 4,
        [own_shape, ((elems, width // face_dofs * inside), BF16)],
        [
            VMEM((elems, width // face_dofs * inside), BF16),
            pltpu.SemaphoreType.DMA((pairs // 2,)),
        ],
        4 * pairs * elems * eld * inside,
        "finish",
        [VMEM, HBM],
    )
    (applied,) = call(
        last_kernel,
        [own, *returned, give],
        [VMEM] * 5,
        [field],
        [
            VMEM((LANES, width), BF16),
            VMEM((faces, width), BF16),
            pltpu.SemaphoreType.DMA((faces // LANES,)),
        ],
        2 * faces * width * 128,
        "last",
        [HBM],
    )
    return (applied, interior)


def solution(mesh):
    rows = P(("grp", "elem", "sub"))
    split = P(("grp", "elem", "sub"), "src")
    in_specs = (
        split,
        rows,
        rows,
        rows,
        P(("grp", "elem", "sub"), None),
        P(("grp", "elem", "sub"), None, None),
        rows,
        P(),
        P(),
        P(),
        P(),
    )
    return jax.shard_map(
        functools.partial(per_device, (mesh.shape["elem"], mesh.shape["sub"])),
        mesh=mesh,
        in_specs=in_specs,
        out_specs=(split, split),
        check_vma=False,
    )
```
